32 devices in a mesh: tm: 4 (over y, core), site: 8 (over z, x).
Axes of the slice: x: 2, y: 2, z: 4, core: 2. Of those that a mesh axis runs over, the one named last changes fastest.
Arguments:
- left_modes: bfloat16 [4, 2, 512, 1536], P('tm', None, None, 'site'), may hold values from -6 to 6
- right_modes: bfloat16 [4, 2, 2048, 1536], P('tm', None, None, 'site'), may hold values from -6 to 6
- momenta: int32 [4, 3], P('tm'), may hold values from -3 to 3
- far_fields: bfloat16 [4, 2, 2048, 2048], P('tm', None, None, 'site'), may hold values from -0.09375 to 0.09375
Outputs:
- meson: bfloat16 [4, 2, 512, 2048], P('tm', None, None, 'site')
- product: bfloat16 [4, 2, 512, 2048], P('tm', None, None, 'site')
The draws below stay inside these ranges and needn't reach their ends.
All inputs are finite; a program needn't handle non-finite values.
Results may differ from the reference program's by a relative error of at most 0.0058.
Values may be sent and summed in bfloat16 or wider, within the bound.
A program may use at most 64 MiB of HBM per device.

```python
import math
import jax
import jax.numpy as jnp
from jax import lax

MODES = 2048
SC = 12
EXTENT = 96
ROWS = 512
DT = 3
SLAB = 128
TIMES = 4


def place_ends(values, rng, low, high):
    longest = values.shape.index(max(values.shape))
    spots = []
    for shift in (0, 1):
        where = [jax.random.randint(jax.random.fold_in(rng, axis), (), 0, length) for axis, length in enumerate(values.shape)]
        where[longest] = (where[longest] + shift) % values.shape[longest]
        spots.append(tuple(where))
    return values.at[spots[0]].set(low).at[spots[1]].set(high)


def with_spikes(drawn, own_key, source, target, blocks, factor):
    owner, partner = [(jnp.arange(drawn.shape[axis_at]) // (drawn.shape[axis_at] // blocks)).reshape([-1 if axis == axis_at else 1 for axis in range(drawn.ndim)]) for axis_at in (source, target)]
    chosen = jax.random.permutation(own_key, blocks)[partner]
    strong = (owner == chosen) | (owner == (partner + blocks // 2) % blocks)
    return jnp.where(strong, factor * drawn, drawn)


def shard_levels(key, shape, shards, least, top_value):
    factor_of, own = 1.0, jax.random.fold_in(key, 6)
    for axis_at, blocks in shards:
        steps = jnp.exp(jax.random.uniform(jax.random.fold_in(own, axis_at), (blocks,), jnp.float32, least / len(shards), top_value / len(shards)))
        factor_of = factor_of * jnp.repeat(steps, shape[axis_at] // blocks).reshape([-1 if axis == axis_at else 1 for axis in range(len(shape))])
    return factor_of


def scatter_about(key, extent, width, most, pieces=(), kind=jnp.bfloat16):
    values = width * jax.random.normal(key, extent, jnp.float32)
    if pieces:
        values = values * shard_levels(key, extent, pieces, -0.22, 0.18)
    return jnp.clip(values, -most, most).astype(kind)


def heavy_noise(key, extent, scale, most, split, heavy, kind=jnp.bfloat16):
    array = scale * jax.random.normal(key, extent, jnp.float32)
    if split:
        array = array * shard_levels(key, extent, split, -0.22, 0.18)
    return jnp.clip(with_spikes(array, jax.random.fold_in(key, 3), *heavy), -most, most).astype(kind)


def setup_inputs(seed: int = 0) -> dict:
    seeds = jax.random.split(jax.random.key(seed), 5)
    return {
        "left_modes": scatter_about(seeds[0], (TIMES, 2, ROWS, SLAB * SC), 1.0, 6.0, ((0, 4), (3, 8))),
        "right_modes": heavy_noise(seeds[1], (TIMES, 2, MODES, SLAB * SC), 1.0, 6.0, ((0, 4), (3, 8)), (3, 2, 8, 2.0)),
        "momenta": place_ends(jax.random.randint(seeds[2], (TIMES, 3), -3, 4), jax.random.fold_in(seeds[2], 1), -3, 3).astype(jnp.int32),
        "far_fields": scatter_about(seeds[3], (TIMES, 2, MODES, MODES), (2 * MODES) ** -0.5, 0.09375, ((0, 4), (3, 8))),
    }


def block_coords(sites):
    coord_x = jnp.zeros_like(sites)
    coord_y = jnp.zeros_like(sites)
    coord_z = jnp.zeros_like(sites)
    for level in range(7):
        coord_x = coord_x + ((sites // (8 ** level)) % 2) * (2 ** level)
        coord_y = coord_y + ((sites // (2 * 8 ** level)) % 2) * (2 ** level)
        coord_z = coord_z + ((sites // (4 * 8 ** level)) % 2) * (2 ** level)
    return coord_x, coord_y, coord_z


def phase_table(momentum):
    sites = jnp.arange(SLAB, dtype=jnp.int32)
    coord_x, coord_y, coord_z = block_coords(sites)
    wave = (momentum[0] * coord_x + momentum[1] * coord_y + momentum[2] * coord_z) % EXTENT
    angles = (2.0 * math.pi / EXTENT) * wave.astype(jnp.float32)
    return jnp.repeat(jnp.cos(angles), SC), jnp.repeat(jnp.sin(angles), SC)


def reference(left_modes, right_modes, momenta, far_fields):
    factor = (24.0 * SLAB) ** -0.5

    def one_slice(slice_index):
        cosine, sine = phase_table(momenta[slice_index])
        left_real = left_modes[slice_index, 0].astype(jnp.float32)
        left_imag = left_modes[slice_index, 1].astype(jnp.float32)
        phased_real = (factor * (left_real * cosine + left_imag * sine)).astype(jnp.bfloat16)
        phased_imag = (factor * (left_real * sine - left_imag * cosine)).astype(jnp.bfloat16)
        right_real = right_modes[slice_index, 0]
        right_imag = right_modes[slice_index, 1]
        meson_real = jnp.dot(phased_real, right_real.T, preferred_element_type=jnp.float32) - jnp.dot(phased_imag, right_imag.T, preferred_element_type=jnp.float32)
        meson_imag = jnp.dot(phased_real, right_imag.T, preferred_element_type=jnp.float32) + jnp.dot(phased_imag, right_real.T, preferred_element_type=jnp.float32)
        meson_block = jnp.stack([meson_real, meson_imag]).astype(jnp.bfloat16)
        later = far_fields[(slice_index + DT) % TIMES]
        prod_real = jnp.dot(meson_block[0], later[0], preferred_element_type=jnp.float32) - jnp.dot(meson_block[1], later[1], preferred_element_type=jnp.float32)
        prod_imag = jnp.dot(meson_block[0], later[1], preferred_element_type=jnp.float32) + jnp.dot(meson_block[1], later[0], preferred_element_type=jnp.float32)
        return meson_block, jnp.stack([prod_real, prod_imag]).astype(jnp.bfloat16)

    meson, product = lax.map(one_slice, jnp.arange(TIMES, dtype=jnp.int32))
    return meson, product
```

```python
import functools
import math

import jax
import jax.numpy as jnp
from jax import lax
from jax.experimental import pallas as pl
from jax.experimental.pallas import tpu as pltpu
from jax.sharding import PartitionSpec as P

SC = 12
EXTENT = 96
DT = 3
PAIR = 2
MESH = pl.DeviceIdType.MESH
NT = (((1,), (1,)), ((), ()))


def block_coords(sites):
    coord_x = jnp.zeros_like(sites)
    coord_y = jnp.zeros_like(sites)
    coord_z = jnp.zeros_like(sites)
    for level in range(7):
        coord_x = coord_x + sites // 8**level % 2 * 2**level
        coord_y = coord_y + sites // (2 * 8**level) % 2 * 2**level
        coord_z = coord_z + sites // (4 * 8**level) % 2 * 2**level
    return (coord_x, coord_y, coord_z)


def order(k, z, nz):
    short = jnp.minimum(z, nz - 1 - z)
    lone = nz - 1 - 2 * short
    toward = jnp.where(z < nz - 1 - z, 1, -1)
    rest = k - lone
    far = z + toward * (nz - 1 - short - k)
    near = z + (short - rest // 2) * (1 - 2 * (rest % 2))
    return jnp.where(k == nz - 1, z, jnp.where(k < lone, far, near))


def kernel(
    times,
    groups,
    factor,
    left_ref,
    right_ref,
    wave_ref,
    far_ref,
    meson_ref,
    product_ref,
    phased,
    field,
    x_out,
    x_in,
    z_out,
    z_in,
    gathered,
    total,
    far_send,
    far_recv,
    xo_sem,
    xi_sem,
    zo_sem,
    zi_sem,
    g_recv,
    g_up,
    g_down,
    g_pair,
):
    nz = groups // PAIR
    cols = meson_ref.shape[2]
    tm = lax.axis_index("tm")
    me = lax.axis_index("site")
    z = me // PAIR
    x = me % PAIR
    mate = z * PAIR + (1 - x)
    up = me + PAIR
    down = me - PAIR
    has_up = z < nz - 1
    has_down = z > 0
    target = lax.rem(tm + times - DT % times, times)
    source = lax.rem(tm + DT, times)

    barrier = pltpu.get_barrier_semaphore()
    pl.semaphore_signal(barrier, inc=1, device_id=(target, me), device_id_type=MESH)
    pl.semaphore_signal(barrier, inc=1, device_id=(source, me), device_id_type=MESH)
    pl.semaphore_signal(barrier, inc=1, device_id=(tm, mate), device_id_type=MESH)

    @pl.when(has_up)
    def _():
        pl.semaphore_signal(barrier, inc=1, device_id=(tm, up), device_id_type=MESH)

    @pl.when(has_down)
    def _():
        pl.semaphore_signal(barrier, inc=1, device_id=(tm, down), device_id_type=MESH)

    pl.semaphore_wait(barrier, 3 + has_up.astype(jnp.int32) + has_down.astype(jnp.int32))

    def send(src, dst, send_sem, recv_sem, site):
        return pltpu.make_async_remote_copy(
            src_ref=src,
            dst_ref=dst,
            send_sem=send_sem,
            recv_sem=recv_sem,
            device_id=(tm, site),
            device_id_type=MESH,
        )

    far_copy = pltpu.make_async_remote_copy(
        src_ref=far_ref,
        dst_ref=field,
        send_sem=far_send,
        recv_sem=far_recv,
        device_id=(target, me),
        device_id_type=MESH,
    )
    far_copy.start()

    cosine = wave_ref[0:1, :]
    sine = wave_ref[1:2, :]
    real = left_ref[0].astype(jnp.float32)
    imag = left_ref[1].astype(jnp.float32)
    phased[0] = (factor * (real * cosine + imag * sine)).astype(jnp.bfloat16)
    phased[1] = (factor * (real * sine - imag * cosine)).astype(jnp.bfloat16)

    def partial(site):
        rows = pl.ds(pl.multiple_of(site * cols, cols), cols)
        right_real = right_ref[0, rows, :]
        right_imag = right_ref[1, rows, :]

        def dot(a, b):
            return lax.dot_general(a, b, NT, preferred_element_type=jnp.float32)

        return (
            dot(phased[0], right_real) - dot(phased[1], right_imag),
            dot(phased[0], right_imag) + dot(phased[1], right_real),
        )

    def x_copy(dest):
        return send(x_out.at[dest], x_in.at[dest], xo_sem.at[dest], xi_sem.at[dest], mate)

    def z_copy(dest, side, site):
        return send(
            z_out.at[dest], z_in.at[dest, side], zo_sem.at[dest], zi_sem.at[dest, side], site
        )

    def first(k, carry):
        dest = order(k, z, nz)
        for part, value in enumerate(partial(dest * PAIR + (1 - x))):
            x_out[dest, part] = value.astype(jnp.bfloat16)
        x_copy(dest).start()
        return carry

    lax.fori_loop(0, nz, first, 0)

    def second(k, carry):
        dest = order(k, z, nz)
        mine = partial(dest * PAIR + x)
        for part in range(2):
            total[part] = mine[part]
        x_copy(dest).wait_recv()
        total[...] += x_in[dest].astype(jnp.float32)

        @pl.when((dest >= z) & has_down)
        def _():
            z_copy(dest, 0, up).wait_recv()
            total[...] += z_in[dest, 0].astype(jnp.float32)

        @pl.when((dest <= z) & has_up)
        def _():
            z_copy(dest, 1, down).wait_recv()
            total[...] += z_in[dest, 1].astype(jnp.float32)

        z_out[dest] = total[...].astype(jnp.bfloat16)

        @pl.when(dest > z)
        def _():
            z_copy(dest, 0, up).start()

        @pl.when(dest < z)
        def _():
            z_copy(dest, 1, down).start()

        return carry

    lax.fori_loop(0, nz, second, 0)

    def block(site):
        return gathered.at[site]

    def to_up(src, site):
        return send(src, block(site), g_up.at[site // PAIR], g_recv.at[site], up)

    def to_down(src, site):
        return send(src, block(site), g_down.at[site // PAIR], g_recv.at[site], down)

    def to_mate(src, site):
        return send(src, block(site), g_pair.at[site // PAIR], g_recv.at[site], mate)

    own = z_out.at[z]

    @pl.when(has_up)
    def _():
        to_up(own, me).start()

    @pl.when(has_down)
    def _():
        to_down(own, me).start()

    to_mate(own, me).start()
    meson_ref[...] = own[...]

    far_copy.wait()

    def gain(value, site):
        rows = pl.ds(pl.multiple_of(site * cols, cols), cols)
        field_real = field[0, rows, :]
        field_imag = field[1, rows, :]

        def dot(a, b):
            return jnp.dot(a, b, preferred_element_type=jnp.float32)

        return (
            dot(value[0], field_real) - dot(value[1], field_imag),
            dot(value[0], field_imag) + dot(value[1], field_real),
        )

    for part, value in enumerate(gain(own, me)):
        total[part] = value

    def arrive(site):
        for part, value in enumerate(gain(block(site), site)):
            total[part] += value

    def relay(d, carry):
        below = me - d * PAIR
        above = me + d * PAIR

        @pl.when(z >= d)
        def _():
            to_up(block(below), below).wait_recv()

            @pl.when(has_up)
            def _():
                to_up(block(below), below).start()

            to_mate(block(below), below).start()

        @pl.when(z + d < nz)
        def _():
            to_down(block(above), above).wait_recv()

            @pl.when(has_down)
            def _():
                to_down(block(above), above).start()

            to_mate(block(above), above).start()

        @pl.when(z >= d)
        def _():
            arrive(below)

        @pl.when(z + d < nz)
        def _():
            arrive(above)

        return carry

    lax.fori_loop(1, nz, relay, 0)

    def across(d, carry):
        @pl.when(z >= d)
        def _():
            site = mate - d * PAIR
            to_mate(block(site), site).wait_recv()
            arrive(site)

        @pl.when((z + d < nz) & (d > 0))
        def _():
            site = mate + d * PAIR
            to_mate(block(site), site).wait_recv()
            arrive(site)

        return carry

    lax.fori_loop(0, nz, across, 0)
    product_ref[...] = total[...].astype(jnp.bfloat16)

    def drain(k, carry):
        x_copy(k).wait_send()

        @pl.when(k != z)
        def _():
            z_copy(k, 0, mate).wait_send()

        to_mate(own, k * PAIR + x).wait_send()

        @pl.when((k <= z) & has_up)
        def _():
            to_up(own, k * PAIR + x).wait_send()

        @pl.when((k >= z) & has_down)
        def _():
            to_down(own, k * PAIR + x).wait_send()

        return carry

    lax.fori_loop(0, nz, drain, 0)


def body(left_modes, right_modes, momenta, far_fields):
    times = lax.axis_size("tm")
    groups = lax.axis_size("site")
    nz = groups // PAIR
    rows, width = left_modes.shape[2:]
    modes, cols = far_fields.shape[2:]
    count = width // SC
    factor = (2.0 * width * groups) ** (-0.5)
    sites = lax.axis_index("site") * count + jnp.arange(count, dtype=jnp.int32)
    momentum = momenta[0]
    coord_x, coord_y, coord_z = block_coords(sites)
    wave = (momentum[0] * coord_x + momentum[1] * coord_y + momentum[2] * coord_z) % EXTENT
    angles = 2.0 * math.pi / EXTENT * wave.astype(jnp.float32)
    waves = jnp.repeat(jnp.stack([jnp.cos(angles), jnp.sin(angles)]), SC, axis=1)
    chunk = (2, rows, cols)
    dma = pltpu.SemaphoreType.DMA
    meson, product = pl.pallas_call(
        functools.partial(kernel, times, groups, factor),
        out_shape=[jax.ShapeDtypeStruct(chunk, jnp.bfloat16)] * 2,
        in_specs=[pl.BlockSpec(memory_space=pltpu.VMEM)] * 3 + [pl.BlockSpec(memory_space=pl.ANY)],
        out_specs=[pl.BlockSpec(memory_space=pltpu.VMEM)] * 2,
        scratch_shapes=[
            pltpu.VMEM((2, rows, width), jnp.bfloat16),
            pltpu.VMEM((2, modes, cols), jnp.bfloat16),
            pltpu.VMEM((nz,) + chunk, jnp.bfloat16),
            pltpu.VMEM((nz,) + chunk, jnp.bfloat16),
            pltpu.VMEM((nz,) + chunk, jnp.bfloat16),
            pltpu.VMEM((nz, 2) + chunk, jnp.bfloat16),
            pltpu.VMEM((groups,) + chunk, jnp.bfloat16),
            pltpu.VMEM(chunk, jnp.float32),
            dma(()),
            dma(()),
            dma((nz,)),
            dma((nz,)),
            dma((nz,)),
            dma((nz, 2)),
            dma((groups,)),
            dma((nz,)),
            dma((nz,)),
            dma((nz,)),
        ],
        compiler_params=pltpu.CompilerParams(
            collective_id=0, has_side_effects=True, vmem_limit_bytes=60 * 2**20
        ),
    )(left_modes[0], right_modes[0], waves, far_fields[0])
    return (meson[None], product[None])


def solution(mesh):
    return jax.shard_map(
        body,
        mesh=mesh,
        in_specs=(
            P("tm", None, None, "site"),
            P("tm", None, None, "site"),
            P("tm", None),
            P("tm", None, None, "site"),
        ),
        out_specs=(P("tm", None, None, "site"), P("tm", None, None, "site")),
        check_vma=False,
    )
```

```python
import functools
import math

import jax
import jax.numpy as jnp
from jax import lax
from jax.experimental import pallas as pl
from jax.experimental.pallas import tpu as pltpu
from jax.sharding import PartitionSpec as P

SC = 12
EXTENT = 96
DT = 3
PAIR = 2
MESH = pl.DeviceIdType.MESH


def block_coords(sites):
    coords = []
    for axis in range(3):
        coord = jnp.zeros_like(sites)
        for level in range(7):
            coord = coord + ((sites >> (3 * level + axis)) & 1) * 2**level
        coords.append(coord)
    return coords


def order(k, z, nz):
    short = jnp.minimum(z, nz - 1 - z)
    lone = nz - 1 - 2 * short
    toward = jnp.where(z < nz - 1 - z, 1, -1)
    rest = k - lone
    far = z + toward * (nz - 1 - short - k)
    near = z + (short - rest // 2) * (1 - 2 * (rest % 2))
    return jnp.where(k == nz - 1, z, jnp.where(k < lone, far, near))


def kernel(
    times,
    groups,
    factor,
    left_ref,
    right_ref,
    momenta_ref,
    far_ref,
    meson_ref,
    product_ref,
    phased,
    field,
    x_out,
    x_in,
    z_out,
    z_in,
    gathered,
    total,
    far_send,
    far_recv,
    xo_sem,
    xi_sem,
    zo_sem,
    zi_sem,
    g_recv,
    g_up,
    g_down,
    g_pair,
    s_recv,
    s_up,
    s_down,
    s_pair,
):
    nz = groups // PAIR
    rows, cols = meson_ref.shape[1:]
    width = left_ref.shape[1]
    thin = max(16, rows // 6 // 16 * 16)
    tm = lax.axis_index("tm")
    me = lax.axis_index("site")
    z = me // PAIR
    x = me % PAIR
    mate = z * PAIR + (1 - x)
    up = me + PAIR
    down = me - PAIR
    has_up = z < nz - 1
    has_down = z > 0
    target = lax.rem(tm + times - DT % times, times)
    source = lax.rem(tm + DT, times)

    barrier = pltpu.get_barrier_semaphore()
    pl.semaphore_signal(barrier, inc=1, device_id=(target, me), device_id_type=MESH)
    pl.semaphore_signal(barrier, inc=1, device_id=(source, me), device_id_type=MESH)
    pl.semaphore_signal(barrier, inc=1, device_id=(tm, mate), device_id_type=MESH)

    @pl.when(has_up)
    def _():
        pl.semaphore_signal(barrier, inc=1, device_id=(tm, up), device_id_type=MESH)

    @pl.when(has_down)
    def _():
        pl.semaphore_signal(barrier, inc=1, device_id=(tm, down), device_id_type=MESH)

    pl.semaphore_wait(barrier, 3 + has_up.astype(jnp.int32) + has_down.astype(jnp.int32))

    def send(src, dst, send_sem, recv_sem, site):
        return pltpu.make_async_remote_copy(
            src_ref=src,
            dst_ref=dst,
            send_sem=send_sem,
            recv_sem=recv_sem,
            device_id=(tm, site),
            device_id_type=MESH,
        )

    far_copy = pltpu.make_async_remote_copy(
        src_ref=far_ref,
        dst_ref=field,
        send_sem=far_send,
        recv_sem=far_recv,
        device_id=(target, me),
        device_id_type=MESH,
    )
    far_copy.start()

    column = lax.broadcasted_iota(jnp.int32, (width, 128), 0)
    inside = jnp.floor((column.astype(jnp.float32) + 0.5) / SC).astype(jnp.int32)
    sites = me * (width // SC) + inside
    coords = block_coords(sites)
    wave = sum(momenta_ref[0, axis] * coords[axis] for axis in range(3)).astype(jnp.float32)
    wave = wave - EXTENT * jnp.floor((wave + 0.5) / EXTENT)
    angles = 2.0 * math.pi / EXTENT * wave
    cosine = jnp.cos(angles)[:, 0:1]
    sine = jnp.sin(angles)[:, 0:1]
    real = left_ref[0].astype(jnp.float32)
    imag = left_ref[1].astype(jnp.float32)
    phased_real = factor * (real * cosine + imag * sine)
    phased_imag = factor * (real * sine - imag * cosine)
    for_real = jnp.concatenate([phased_real, -phased_imag], axis=0)
    for_imag = jnp.concatenate([phased_imag, phased_real], axis=0)
    phased[0:rows, :] = for_real.T.astype(jnp.bfloat16)
    phased[rows : 2 * rows, :] = for_imag.T.astype(jnp.bfloat16)

    def partial(site):
        lanes = pl.ds(pl.multiple_of(site * cols, cols), cols)
        right = right_ref[:, :, lanes].reshape(2 * width, cols)
        both = jnp.dot(phased[...], right, preferred_element_type=jnp.float32)
        return both.reshape(2, rows, cols)

    def x_copy(dest):
        return send(x_out.at[dest], x_in.at[dest], xo_sem.at[dest], xi_sem.at[dest], mate)

    def z_copy(dest, side, site):
        return send(
            z_out.at[dest], z_in.at[dest, side], zo_sem.at[dest], zi_sem.at[dest, side], site
        )

    def first(k, carry):
        dest = order(k, z, nz)
        x_out[dest] = partial(dest * PAIR + (1 - x)).astype(jnp.bfloat16)
        x_copy(dest).start()
        return carry

    lax.fori_loop(0, nz, first, 0)

    def second(k, carry):
        dest = order(k, z, nz)
        total[...] = partial(dest * PAIR + x)
        x_copy(dest).wait_recv()
        total[...] += x_in[dest].astype(jnp.float32)

        @pl.when((dest >= z) & has_down)
        def _():
            z_copy(dest, 0, up).wait_recv()
            total[...] += z_in[dest, 0].astype(jnp.float32)

        @pl.when((dest <= z) & has_up)
        def _():
            z_copy(dest, 1, down).wait_recv()
            total[...] += z_in[dest, 1].astype(jnp.float32)

        z_out[dest] = total[...].astype(jnp.bfloat16)

        @pl.when(dest > z)
        def _():
            z_copy(dest, 0, up).start()

        @pl.when(dest < z)
        def _():
            z_copy(dest, 1, down).start()

        return carry

    lax.fori_loop(0, nz, second, 0)

    def block(site):
        return gathered.at[site]

    def to_up(src, site):
        return send(src, block(site), g_up.at[site // PAIR], g_recv.at[site], up)

    def to_down(src, site):
        return send(src, block(site), g_down.at[site // PAIR], g_recv.at[site], down)

    def slim(ref):
        return ref.at[:, pl.ds(0, thin), :]

    def rest(ref):
        return ref.at[:, pl.ds(thin, rows - thin), :]

    def to_mate(src, site):
        return send(
            rest(src), rest(block(site)), g_pair.at[site // PAIR], g_recv.at[site], mate
        )

    def slim_up(site):
        part = slim(block(site))
        return send(part, part, s_up.at[site // PAIR], s_recv.at[site], up)

    def slim_down(site):
        part = slim(block(site))
        return send(part, part, s_down.at[site // PAIR], s_recv.at[site], down)

    def slim_mate(src, site):
        return send(slim(src), slim(block(site)), s_pair, s_recv.at[site], mate)

    own = z_out.at[z]
    slim_mate(own, me).start()

    @pl.when(has_up)
    def _():
        to_up(own, me).start()

    @pl.when(has_down)
    def _():
        to_down(own, me).start()

    to_mate(own, me).start()
    meson_ref[...] = own[...]
    slim_mate(block(mate), mate).wait_recv()

    @pl.when(has_up)
    def _():
        slim_up(mate).start()

    @pl.when(has_down)
    def _():
        slim_down(mate).start()

    far_copy.wait()

    def gain(value, site):
        lines = pl.ds(pl.multiple_of(site * cols, cols), cols)
        both = value[...].reshape(2 * rows, cols)

        def dot(part):
            whole = jnp.dot(both, field[part, lines, :], preferred_element_type=jnp.float32)
            return whole[:rows], whole[rows:]

        real_real, imag_real = dot(0)
        real_imag, imag_imag = dot(1)
        return (real_real - imag_imag, real_imag + imag_real)

    for part, value in enumerate(gain(own, me)):
        total[part] = value

    def arrive(site):
        for part, value in enumerate(gain(block(site), site)):
            total[part] += value

    def relay(d, carry):
        below = me - d * PAIR
        above = me + d * PAIR

        @pl.when(z >= d)
        def _():
            to_up(block(below), below).wait_recv()

            @pl.when(has_up)
            def _():
                to_up(block(below), below).start()

            to_mate(block(below), below).start()

        @pl.when(z + d < nz)
        def _():
            to_down(block(above), above).wait_recv()

            @pl.when(has_down)
            def _():
                to_down(block(above), above).start()

            to_mate(block(above), above).start()

        @pl.when(z >= d)
        def _():
            arrive(below)

        @pl.when(z + d < nz)
        def _():
            arrive(above)

        @pl.when(z >= d)
        def _():
            site = mate - d * PAIR
            slim_up(site).wait_recv()

            @pl.when(has_up)
            def _():
                slim_up(site).start()

        @pl.when(z + d < nz)
        def _():
            site = mate + d * PAIR
            slim_down(site).wait_recv()

            @pl.when(has_down)
            def _():
                slim_down(site).start()

        return carry

    lax.fori_loop(1, nz, relay, 0)

    def across(d, carry):
        @pl.when(z >= d)
        def _():
            site = mate - d * PAIR
            to_mate(block(site), site).wait_recv()
            arrive(site)

        @pl.when((z + d < nz) & (d > 0))
        def _():
            site = mate + d * PAIR
            to_mate(block(site), site).wait_recv()
            arrive(site)

        return carry

    lax.fori_loop(0, nz, across, 0)
    product_ref[...] = total[...].astype(jnp.bfloat16)

    def drain(k, carry):
        x_copy(k).wait_send()

        @pl.when(k != z)
        def _():
            z_copy(k, 0, mate).wait_send()

        to_mate(own, k * PAIR + x).wait_send()

        @pl.when((k <= z) & has_up)
        def _():
            to_up(own, k * PAIR + x).wait_send()
            slim_up(k * PAIR + 1 - x).wait_send()

        @pl.when((k >= z) & has_down)
        def _():
            to_down(own, k * PAIR + x).wait_send()
            slim_down(k * PAIR + 1 - x).wait_send()

        return carry

    lax.fori_loop(0, nz, drain, 0)
    slim_mate(own, me).wait_send()


def settle(meson_in, product_in, meson_ref, product_ref):
    meson_ref[...] = meson_in[...]
    product_ref[...] = product_in[...]


def body(left_modes, right_modes, momenta, far_fields):
    times = lax.axis_size("tm")
    groups = lax.axis_size("site")
    nz = groups // PAIR
    rows, width = left_modes.shape[2:]
    modes, cols = far_fields.shape[2:]
    factor = (2.0 * width * groups) ** (-0.5)
    chunk = (2, rows, cols)
    dma = pltpu.SemaphoreType.DMA
    meson, product = pl.pallas_call(
        functools.partial(kernel, times, groups, factor),
        out_shape=[jax.ShapeDtypeStruct(chunk, jnp.bfloat16)] * 2,
        in_specs=[
            pl.BlockSpec(memory_space=pltpu.VMEM),
            pl.BlockSpec(memory_space=pltpu.VMEM),
            pl.BlockSpec(memory_space=pltpu.SMEM),
            pl.BlockSpec(memory_space=pl.ANY),
        ],
        out_specs=[pl.BlockSpec(memory_space=pltpu.VMEM)] * 2,
        scratch_shapes=[
            pltpu.VMEM((2 * rows, 2 * width), jnp.bfloat16),
            pltpu.VMEM((2, modes, cols), jnp.bfloat16),
            pltpu.VMEM((nz,) + chunk, jnp.bfloat16),
            pltpu.VMEM((nz,) + chunk, jnp.bfloat16),
            pltpu.VMEM((nz,) + chunk, jnp.bfloat16),
            pltpu.VMEM((nz, 2) + chunk, jnp.bfloat16),
            pltpu.VMEM((groups,) + chunk, jnp.bfloat16),
            pltpu.VMEM(chunk, jnp.float32),
            dma(()),
            dma(()),
            dma((nz,)),
            dma((nz,)),
            dma((nz,)),
            dma((nz, 2)),
            dma((groups,)),
            dma((nz,)),
            dma((nz,)),
            dma((nz,)),
            dma((groups,)),
            dma((nz,)),
            dma((nz,)),
            dma(()),
        ],
        compiler_params=pltpu.CompilerParams(
            collective_id=0, has_side_effects=True, vmem_limit_bytes=60 * 2**20
        ),
    )(
        jnp.swapaxes(left_modes[0], 1, 2),
        jnp.swapaxes(right_modes[0], 1, 2),
        momenta,
        far_fields[0],
    )
    meson, product = pl.pallas_call(
        settle,
        out_shape=[jax.ShapeDtypeStruct(chunk, jnp.bfloat16)] * 2,
        in_specs=[pl.BlockSpec(memory_space=pltpu.VMEM)] * 2,
        out_specs=[pl.BlockSpec(memory_space=pltpu.VMEM)] * 2,
        compiler_params=pltpu.CompilerParams(vmem_limit_bytes=16 * 2**20),
    )(meson, product)
    return (meson[None], product[None])


def solution(mesh):
    return jax.shard_map(
        body,
        mesh=mesh,
        in_specs=(
            P("tm", None, None, "site"),
            P("tm", None, None, "site"),
            P("tm", None),
            P("tm", None, None, "site"),
        ),
        out_specs=(P("tm", None, None, "site"), P("tm", None, None, "site")),
        check_vma=False,
    )
```

```python
import functools
import math

import jax
import jax.numpy as jnp
from jax import lax
from jax.experimental import pallas as pl
from jax.experimental.pallas import tpu as pltpu
from jax.sharding import PartitionSpec as P

SC = 12
EXTENT = 96
DT = 3
PAIR = 2
MESH = pl.DeviceIdType.MESH


def block_coords(sites):
    coords = []
    for axis in range(3):
        coord = jnp.zeros_like(sites)
        for level in range(7):
            coord = coord + ((sites >> (3 * level + axis)) & 1) * 2**level
        coords.append(coord)
    return coords


def thin_rows(rows):
    return max(16, rows // 6 // 16 * 16)


def order(k, z, nz):
    short = jnp.minimum(z, nz - 1 - z)
    lone = nz - 1 - 2 * short
    toward = jnp.where(z < nz - 1 - z, 1, -1)
    rest = k - lone
    far = z + toward * (nz - 1 - short - k)
    near = z + (short - rest // 2) * (1 - 2 * (rest % 2))
    return jnp.where(k == nz - 1, z, jnp.where(k < lone, far, near))


def kernel(
    times,
    groups,
    factor,
    left_ref,
    right_ref,
    momenta_ref,
    far_ref,
    meson_ref,
    product_ref,
    phased,
    field,
    x_out,
    x_in,
    z_out,
    z_in,
    gathered,
    total,
    far_send,
    far_recv,
    xo_sem,
    xi_sem,
    zo_sem,
    zi_sem,
    g_recv,
    g_up,
    g_down,
    g_pair,
    s_recv,
    s_up,
    s_down,
    s_pair,
    left_in,
    right_in,
    left_sem,
    right_sem,
    kept,
    t_out,
    t_in,
    to_sem,
    ti_sem,
    m_out,
    m_in,
    m_sem,
    mine,
):
    nz = groups // PAIR
    rows, cols = meson_ref.shape[1:]
    width = left_ref.shape[1]
    thin = thin_rows(rows)
    tm = lax.axis_index("tm")
    me = lax.axis_index("site")
    z = me // PAIR
    x = me % PAIR
    mate = z * PAIR + (1 - x)
    up = me + PAIR
    down = me - PAIR
    has_up = z < nz - 1
    has_down = z > 0
    target = lax.rem(tm + times - DT % times, times)
    source = lax.rem(tm + DT, times)

    left_copy = pltpu.make_async_copy(left_ref, left_in, left_sem)
    left_copy.start()

    def right_copy(site):
        lanes = pl.ds(pl.multiple_of(site * cols, cols), cols)
        return pltpu.make_async_copy(right_ref.at[:, :, lanes], right_in.at[site], right_sem.at[site])

    def load(k, carry):
        dest = order(k, z, nz)
        right_copy(dest * PAIR + (1 - x)).start()
        right_copy(dest * PAIR + x).start()
        return carry

    lax.fori_loop(0, nz, load, 0)

    barrier = pltpu.get_barrier_semaphore()
    pl.semaphore_signal(barrier, inc=1, device_id=(target, me), device_id_type=MESH)
    pl.semaphore_signal(barrier, inc=1, device_id=(source, me), device_id_type=MESH)
    pl.semaphore_signal(barrier, inc=1, device_id=(tm, mate), device_id_type=MESH)

    @pl.when(has_up)
    def _():
        pl.semaphore_signal(barrier, inc=1, device_id=(tm, up), device_id_type=MESH)

    @pl.when(has_down)
    def _():
        pl.semaphore_signal(barrier, inc=1, device_id=(tm, down), device_id_type=MESH)

    def send(src, dst, send_sem, recv_sem, site):
        return pltpu.make_async_remote_copy(
            src_ref=src,
            dst_ref=dst,
            send_sem=send_sem,
            recv_sem=recv_sem,
            device_id=(tm, site),
            device_id_type=MESH,
        )

    column = lax.broadcasted_iota(jnp.int32, (width, 128), 0)
    inside = jnp.floor((column.astype(jnp.float32) + 0.5) / SC).astype(jnp.int32)
    sites = me * (width // SC) + inside
    coords = block_coords(sites)
    wave = sum(momenta_ref[0, axis] * coords[axis] for axis in range(3)).astype(jnp.float32)
    wave = wave - EXTENT * jnp.floor((wave + 0.5) / EXTENT)
    angles = 2.0 * math.pi / EXTENT * wave
    cosine = jnp.cos(angles)[:, 0:1]
    sine = jnp.sin(angles)[:, 0:1]
    left_copy.wait()
    real = left_in[0].astype(jnp.float32)
    imag = left_in[1].astype(jnp.float32)
    phased_real = factor * (real * cosine + imag * sine)
    phased_imag = factor * (real * sine - imag * cosine)
    for_real = jnp.concatenate([phased_real, -phased_imag], axis=0)
    for_imag = jnp.concatenate([phased_imag, phased_real], axis=0)
    phased[0:rows, :] = for_real.T.astype(jnp.bfloat16)
    phased[rows : 2 * rows, :] = for_imag.T.astype(jnp.bfloat16)

    pl.semaphore_wait(barrier, 3 + has_up.astype(jnp.int32) + has_down.astype(jnp.int32))

    far_copy = pltpu.make_async_remote_copy(
        src_ref=far_ref,
        dst_ref=field,
        send_sem=far_send,
        recv_sem=far_recv,
        device_id=(target, me),
        device_id_type=MESH,
    )
    far_copy.start()

    def partial(site):
        right_copy(site).wait()
        right = right_in[site].reshape(2 * width, cols)
        both = jnp.dot(phased[...], right, preferred_element_type=jnp.float32)
        return both.reshape(2, rows, cols)

    def x_copy(dest):
        return send(x_out.at[dest], x_in.at[dest], xo_sem.at[dest], xi_sem.at[dest], mate)

    def z_copy(dest, side, site):
        return send(
            z_out.at[dest], z_in.at[dest, side], zo_sem.at[dest], zi_sem.at[dest, side], site
        )

    def t_copy(dest, side, site):
        return send(
            t_out.at[dest], t_in.at[dest, side], to_sem.at[dest], ti_sem.at[dest, side], site
        )

    m_copy = send(m_out, m_in, m_sem.at[0], m_sem.at[1], mate)

    def first(k, carry):
        dest = order(k, z, nz)
        theirs = partial(dest * PAIR + (1 - x))
        x_out[dest] = theirs[:, thin:].astype(jnp.bfloat16)
        x_copy(dest).start()
        kept[dest, 1, :, :thin] = theirs[:, :thin]
        kept[dest, 0] = partial(dest * PAIR + x)

        @pl.when((dest > z) & has_down)
        def _():
            t_copy(dest, 0, up).wait_recv()
            kept[dest, :, :, :thin] += t_in[dest, 0].astype(jnp.float32)

        @pl.when((dest < z) & has_up)
        def _():
            t_copy(dest, 1, down).wait_recv()
            kept[dest, :, :, :thin] += t_in[dest, 1].astype(jnp.float32)

        @pl.when(dest > z)
        def _():
            t_out[dest] = kept[dest, :, :, :thin].astype(jnp.bfloat16)
            t_copy(dest, 0, up).start()

        @pl.when(dest < z)
        def _():
            t_out[dest] = kept[dest, :, :, :thin].astype(jnp.bfloat16)
            t_copy(dest, 1, down).start()

        return carry

    lax.fori_loop(0, nz, first, 0)

    def second(k, carry):
        dest = order(k, z, nz)
        x_copy(dest).wait_recv()
        kept[dest, 0, :, thin:] += x_in[dest].astype(jnp.float32)

        @pl.when((dest >= z) & has_down)
        def _():
            z_copy(dest, 0, up).wait_recv()
            kept[dest, 0, :, thin:] += z_in[dest, 0].astype(jnp.float32)

        @pl.when((dest <= z) & has_up)
        def _():
            z_copy(dest, 1, down).wait_recv()
            kept[dest, 0, :, thin:] += z_in[dest, 1].astype(jnp.float32)

        @pl.when(dest > z)
        def _():
            z_out[dest] = kept[dest, 0, :, thin:].astype(jnp.bfloat16)
            z_copy(dest, 0, up).start()

        @pl.when(dest < z)
        def _():
            z_out[dest] = kept[dest, 0, :, thin:].astype(jnp.bfloat16)
            z_copy(dest, 1, down).start()

        @pl.when(k == 0)
        def _():
            @pl.when(has_down)
            def _():
                t_copy(z, 0, up).wait_recv()
                kept[z, :, :, :thin] += t_in[z, 0].astype(jnp.float32)

            @pl.when(has_up)
            def _():
                t_copy(z, 1, down).wait_recv()
                kept[z, :, :, :thin] += t_in[z, 1].astype(jnp.float32)

            m_out[...] = kept[z, 1, :, :thin].astype(jnp.bfloat16)
            m_copy.start()

        return carry

    lax.fori_loop(0, nz, second, 0)
    m_copy.wait_recv()
    kept[z, 0, :, :thin] += m_in[...].astype(jnp.float32)
    mine[...] = kept[z, 0].astype(jnp.bfloat16)

    def block(site):
        return gathered.at[site]

    def to_up(src, site):
        return send(src, block(site), g_up.at[site // PAIR], g_recv.at[site], up)

    def to_down(src, site):
        return send(src, block(site), g_down.at[site // PAIR], g_recv.at[site], down)

    def slim(ref):
        return ref.at[:, pl.ds(0, thin), :]

    def rest(ref):
        return ref.at[:, pl.ds(thin, rows - thin), :]

    def to_mate(src, site):
        return send(
            rest(src), rest(block(site)), g_pair.at[site // PAIR], g_recv.at[site], mate
        )

    def slim_up(site):
        part = slim(block(site))
        return send(part, part, s_up.at[site // PAIR], s_recv.at[site], up)

    def slim_down(site):
        part = slim(block(site))
        return send(part, part, s_down.at[site // PAIR], s_recv.at[site], down)

    def slim_mate(src, site):
        return send(slim(src), slim(block(site)), s_pair, s_recv.at[site], mate)

    own = mine
    slim_mate(own, me).start()

    @pl.when(has_up)
    def _():
        to_up(own, me).start()

    @pl.when(has_down)
    def _():
        to_down(own, me).start()

    to_mate(own, me).start()
    meson_ref[...] = own[...]
    slim_mate(block(mate), mate).wait_recv()

    @pl.when(has_up)
    def _():
        slim_up(mate).start()

    @pl.when(has_down)
    def _():
        slim_down(mate).start()

    far_copy.wait()

    def gain(value, site):
        lines = pl.ds(pl.multiple_of(site * cols, cols), cols)
        both = value[...].reshape(2 * rows, cols)

        def dot(part):
            whole = jnp.dot(both, field[part, lines, :], preferred_element_type=jnp.float32)
            return whole[:rows], whole[rows:]

        real_real, imag_real = dot(0)
        real_imag, imag_imag = dot(1)
        return (real_real - imag_imag, real_imag + imag_real)

    for part, value in enumerate(gain(own, me)):
        total[part] = value

    def arrive(site):
        for part, value in enumerate(gain(block(site), site)):
            total[part] += value

    def relay(d, carry):
        below = me - d * PAIR
        above = me + d * PAIR

        @pl.when(z >= d)
        def _():
            to_up(block(below), below).wait_recv()

            @pl.when(has_up)
            def _():
                to_up(block(below), below).start()

            to_mate(block(below), below).start()

        @pl.when(z + d < nz)
        def _():
            to_down(block(above), above).wait_recv()

            @pl.when(has_down)
            def _():
                to_down(block(above), above).start()

            to_mate(block(above), above).start()

        @pl.when(z >= d)
        def _():
            arrive(below)

        @pl.when(z + d < nz)
        def _():
            arrive(above)

        @pl.when(z >= d)
        def _():
            site = mate - d * PAIR
            slim_up(site).wait_recv()

            @pl.when(has_up)
            def _():
                slim_up(site).start()

        @pl.when(z + d < nz)
        def _():
            site = mate + d * PAIR
            slim_down(site).wait_recv()

            @pl.when(has_down)
            def _():
                slim_down(site).start()

        return carry

    lax.fori_loop(1, nz, relay, 0)

    def across(d, carry):
        @pl.when(z >= d)
        def _():
            site = mate - d * PAIR
            to_mate(block(site), site).wait_recv()
            arrive(site)

        @pl.when((z + d < nz) & (d > 0))
        def _():
            site = mate + d * PAIR
            to_mate(block(site), site).wait_recv()
            arrive(site)

        return carry

    lax.fori_loop(0, nz, across, 0)
    product_ref[...] = total[...].astype(jnp.bfloat16)

    def drain(k, carry):
        x_copy(k).wait_send()

        @pl.when(k != z)
        def _():
            z_copy(k, 0, mate).wait_send()
            t_copy(k, 0, mate).wait_send()

        to_mate(own, k * PAIR + x).wait_send()

        @pl.when((k <= z) & has_up)
        def _():
            to_up(own, k * PAIR + x).wait_send()
            slim_up(k * PAIR + 1 - x).wait_send()

        @pl.when((k >= z) & has_down)
        def _():
            to_down(own, k * PAIR + x).wait_send()
            slim_down(k * PAIR + 1 - x).wait_send()

        return carry

    lax.fori_loop(0, nz, drain, 0)
    slim_mate(own, me).wait_send()
    m_copy.wait_send()


def settle(meson_in, product_in, meson_ref, product_ref, held, in_sem, out_sem):
    parts = meson_in.shape[0]
    pairs = [(meson_in, meson_ref), (product_in, product_ref)]
    into, out = [], []
    for which, (src, dst) in enumerate(pairs):
        for part in range(parts):
            slot = which * parts + part
            into.append(pltpu.make_async_copy(src.at[part], held.at[slot], in_sem.at[slot]))
            out.append(pltpu.make_async_copy(held.at[slot], dst.at[part], out_sem.at[slot]))
    for copy in into:
        copy.start()
    for arrived, copy in zip(into, out):
        arrived.wait()
        copy.start()
    for copy in out:
        copy.wait()


def body(left_modes, right_modes, momenta, far_fields):
    times = lax.axis_size("tm")
    groups = lax.axis_size("site")
    nz = groups // PAIR
    rows, width = left_modes.shape[2:]
    modes, cols = far_fields.shape[2:]
    factor = (2.0 * width * groups) ** (-0.5)
    chunk = (2, rows, cols)
    thin = thin_rows(rows)
    large = (2, rows - thin, cols)
    small = (2, thin, cols)
    dma = pltpu.SemaphoreType.DMA
    meson, product = pl.pallas_call(
        functools.partial(kernel, times, groups, factor),
        out_shape=[jax.ShapeDtypeStruct(chunk, jnp.bfloat16)] * 2,
        in_specs=[
            pl.BlockSpec(memory_space=pl.ANY),
            pl.BlockSpec(memory_space=pl.ANY),
            pl.BlockSpec(memory_space=pltpu.SMEM),
            pl.BlockSpec(memory_space=pl.ANY),
        ],
        out_specs=[pl.BlockSpec(memory_space=pltpu.VMEM)] * 2,
        scratch_shapes=[
            pltpu.VMEM((2 * rows, 2 * width), jnp.bfloat16),
            pltpu.VMEM((2, modes, cols), jnp.bfloat16),
            pltpu.VMEM((nz,) + large, jnp.bfloat16),
            pltpu.VMEM((nz,) + large, jnp.bfloat16),
            pltpu.VMEM((nz,) + large, jnp.bfloat16),
            pltpu.VMEM((nz, 2) + large, jnp.bfloat16),
            pltpu.VMEM((groups,) + chunk, jnp.bfloat16),
            pltpu.VMEM(chunk, jnp.float32),
            dma(()),
            dma(()),
            dma((nz,)),
            dma((nz,)),
            dma((nz,)),
            dma((nz, 2)),
            dma((groups,)),
            dma((nz,)),
            dma((nz,)),
            dma((nz,)),
            dma((groups,)),
            dma((nz,)),
            dma((nz,)),
            dma(()),
            pltpu.VMEM((2, width, rows), jnp.bfloat16),
            pltpu.VMEM((groups, 2, width, cols), jnp.bfloat16),
            dma(()),
            dma((groups,)),
            pltpu.VMEM((nz, PAIR) + chunk, jnp.float32),
            pltpu.VMEM((nz, PAIR) + small, jnp.bfloat16),
            pltpu.VMEM((nz, 2, PAIR) + small, jnp.bfloat16),
            dma((nz,)),
            dma((nz, 2)),
            pltpu.VMEM(small, jnp.bfloat16),
            pltpu.VMEM(small, jnp.bfloat16),
            dma((2,)),
            pltpu.VMEM(chunk, jnp.bfloat16),
        ],
        compiler_params=pltpu.CompilerParams(
            collective_id=0, has_side_effects=True, vmem_limit_bytes=60 * 2**20
        ),
    )(
        jnp.swapaxes(left_modes[0], 1, 2),
        jnp.swapaxes(right_modes[0], 1, 2),
        momenta,
        far_fields[0],
    )
    meson, product = pl.pallas_call(
        settle,
        out_shape=[jax.ShapeDtypeStruct(chunk, jnp.bfloat16)] * 2,
        in_specs=[pl.BlockSpec(memory_space=pl.ANY)] * 2,
        out_specs=[pl.BlockSpec(memory_space=pl.ANY)] * 2,
        scratch_shapes=[pltpu.VMEM((4, rows, cols), jnp.bfloat16), dma((4,)), dma((4,))],
        compiler_params=pltpu.CompilerParams(vmem_limit_bytes=60 * 2**20),
    )(meson, product)
    return (meson[None], product[None])


def solution(mesh):
    return jax.shard_map(
        body,
        mesh=mesh,
        in_specs=(
            P("tm", None, None, "site"),
            P("tm", None, None, "site"),
            P("tm", None),
            P("tm", None, None, "site"),
        ),
        out_specs=(P("tm", None, None, "site"), P("tm", None, None, "site")),
        check_vma=False,
    )
```

```python
import functools
import math

import jax
import jax.numpy as jnp
from jax import lax
from jax.experimental import pallas as pl
from jax.experimental.pallas import tpu as pltpu
from jax.sharding import PartitionSpec as P

SC = 12
EXTENT = 96
DT = 3
PAIR = 2
MESH = pl.DeviceIdType.MESH


def block_coords(sites):
    coords = []
    for axis in range(3):
        coord = jnp.zeros_like(sites)
        for level in range(7):
            coord = coord + ((sites >> (3 * level + axis)) & 1) * 2**level
        coords.append(coord)
    return coords


def thin_rows(rows):
    return max(16, rows // 6 // 16 * 16)


def order(k, z, nz):
    short = jnp.minimum(z, nz - 1 - z)
    lone = nz - 1 - 2 * short
    toward = jnp.where(z < nz - 1 - z, 1, -1)
    rest = k - lone
    far = z + toward * (nz - 1 - short - k)
    near = z + (short - rest // 2) * (1 - 2 * (rest % 2))
    return jnp.where(k == nz - 1, z, jnp.where(k < lone, far, near))


def kernel(
    times,
    groups,
    factor,
    left_ref,
    right_ref,
    momenta_ref,
    far_ref,
    meson_ref,
    product_ref,
    phased,
    field,
    x_out,
    x_in,
    z_out,
    z_in,
    gathered,
    total,
    far_send,
    far_recv,
    xo_sem,
    xi_sem,
    zo_sem,
    zi_sem,
    g_recv,
    g_up,
    g_down,
    g_pair,
    s_recv,
    s_up,
    s_down,
    s_pair,
    left_in,
    right_in,
    left_sem,
    right_sem,
    kept,
    t_out,
    t_in,
    to_sem,
    ti_sem,
    m_out,
    m_in,
    m_sem,
    staged,
    leave,
):
    nz = groups // PAIR
    rows, cols = meson_ref.shape[1:]
    width = left_ref.shape[1]
    thin = thin_rows(rows)
    tm = lax.axis_index("tm")
    me = lax.axis_index("site")
    z = me // PAIR
    x = me % PAIR
    mate = z * PAIR + (1 - x)
    up = me + PAIR
    down = me - PAIR
    has_up = z < nz - 1
    has_down = z > 0
    target = lax.rem(tm + times - DT % times, times)
    source = lax.rem(tm + DT, times)

    left_copy = pltpu.make_async_copy(left_ref, left_in, left_sem)
    left_copy.start()

    def right_copy(site):
        lanes = pl.ds(pl.multiple_of(site * cols, cols), cols)
        return pltpu.make_async_copy(right_ref.at[:, :, lanes], right_in.at[site], right_sem.at[site])

    def load(k, carry):
        dest = order(k, z, nz)
        right_copy(dest * PAIR + (1 - x)).start()
        right_copy(dest * PAIR + x).start()
        return carry

    lax.fori_loop(0, nz, load, 0)

    barrier = pltpu.get_barrier_semaphore()
    pl.semaphore_signal(barrier, inc=1, device_id=(target, me), device_id_type=MESH)
    pl.semaphore_signal(barrier, inc=1, device_id=(source, me), device_id_type=MESH)
    pl.semaphore_signal(barrier, inc=1, device_id=(tm, mate), device_id_type=MESH)

    @pl.when(has_up)
    def _():
        pl.semaphore_signal(barrier, inc=1, device_id=(tm, up), device_id_type=MESH)

    @pl.when(has_down)
    def _():
        pl.semaphore_signal(barrier, inc=1, device_id=(tm, down), device_id_type=MESH)

    def send(src, dst, send_sem, recv_sem, site):
        return pltpu.make_async_remote_copy(
            src_ref=src,
            dst_ref=dst,
            send_sem=send_sem,
            recv_sem=recv_sem,
            device_id=(tm, site),
            device_id_type=MESH,
        )

    column = lax.broadcasted_iota(jnp.int32, (width, 128), 0)
    inside = jnp.floor((column.astype(jnp.float32) + 0.5) / SC).astype(jnp.int32)
    sites = me * (width // SC) + inside
    coords = block_coords(sites)
    wave = sum(momenta_ref[0, axis] * coords[axis] for axis in range(3)).astype(jnp.float32)
    wave = wave - EXTENT * jnp.floor((wave + 0.5) / EXTENT)
    angles = 2.0 * math.pi / EXTENT * wave
    cosine = jnp.cos(angles)[:, 0:1]
    sine = jnp.sin(angles)[:, 0:1]
    left_copy.wait()
    real = left_in[0].astype(jnp.float32)
    imag = left_in[1].astype(jnp.float32)
    phased_real = factor * (real * cosine + imag * sine)
    phased_imag = factor * (real * sine - imag * cosine)
    for_real = jnp.concatenate([phased_real, -phased_imag], axis=0)
    for_imag = jnp.concatenate([phased_imag, phased_real], axis=0)
    phased[0:rows, :] = for_real.T.astype(jnp.bfloat16)
    phased[rows : 2 * rows, :] = for_imag.T.astype(jnp.bfloat16)

    pl.semaphore_wait(barrier, 3 + has_up.astype(jnp.int32) + has_down.astype(jnp.int32))

    far_copy = pltpu.make_async_remote_copy(
        src_ref=far_ref,
        dst_ref=field,
        send_sem=far_send,
        recv_sem=far_recv,
        device_id=(target, me),
        device_id_type=MESH,
    )
    far_copy.start()

    def partial(site):
        right_copy(site).wait()
        right = right_in[site].reshape(2 * width, cols)
        both = jnp.dot(phased[...], right, preferred_element_type=jnp.float32)
        return both.reshape(2, rows, cols)

    def x_copy(dest):
        return send(x_out.at[dest], x_in.at[dest], xo_sem.at[dest], xi_sem.at[dest], mate)

    def z_copy(dest, side, site):
        return send(
            z_out.at[dest], z_in.at[dest, side], zo_sem.at[dest], zi_sem.at[dest, side], site
        )

    def t_copy(dest, side, site):
        return send(
            t_out.at[dest], t_in.at[dest, side], to_sem.at[dest], ti_sem.at[dest, side], site
        )

    m_copy = send(m_out, m_in, m_sem.at[0], m_sem.at[1], mate)

    def first(k, carry):
        dest = order(k, z, nz)
        theirs = partial(dest * PAIR + (1 - x))
        x_out[dest] = theirs[:, thin:].astype(jnp.bfloat16)
        x_copy(dest).start()
        kept[dest, 1, :, :thin] = theirs[:, :thin]
        kept[dest, 0] = partial(dest * PAIR + x)

        @pl.when((dest > z) & has_down)
        def _():
            t_copy(dest, 0, up).wait_recv()
            kept[dest, :, :, :thin] += t_in[dest, 0].astype(jnp.float32)

        @pl.when((dest < z) & has_up)
        def _():
            t_copy(dest, 1, down).wait_recv()
            kept[dest, :, :, :thin] += t_in[dest, 1].astype(jnp.float32)

        @pl.when(dest > z)
        def _():
            t_out[dest] = kept[dest, :, :, :thin].astype(jnp.bfloat16)
            t_copy(dest, 0, up).start()

        @pl.when(dest < z)
        def _():
            t_out[dest] = kept[dest, :, :, :thin].astype(jnp.bfloat16)
            t_copy(dest, 1, down).start()

        return carry

    lax.fori_loop(0, nz, first, 0)

    def second(k, carry):
        dest = order(k, z, nz)
        x_copy(dest).wait_recv()
        kept[dest, 0, :, thin:] += x_in[dest].astype(jnp.float32)

        @pl.when((dest >= z) & has_down)
        def _():
            z_copy(dest, 0, up).wait_recv()
            kept[dest, 0, :, thin:] += z_in[dest, 0].astype(jnp.float32)

        @pl.when((dest <= z) & has_up)
        def _():
            z_copy(dest, 1, down).wait_recv()
            kept[dest, 0, :, thin:] += z_in[dest, 1].astype(jnp.float32)

        @pl.when(dest > z)
        def _():
            z_out[dest] = kept[dest, 0, :, thin:].astype(jnp.bfloat16)
            z_copy(dest, 0, up).start()

        @pl.when(dest < z)
        def _():
            z_out[dest] = kept[dest, 0, :, thin:].astype(jnp.bfloat16)
            z_copy(dest, 1, down).start()

        @pl.when(k == 0)
        def _():
            @pl.when(has_down)
            def _():
                t_copy(z, 0, up).wait_recv()
                kept[z, :, :, :thin] += t_in[z, 0].astype(jnp.float32)

            @pl.when(has_up)
            def _():
                t_copy(z, 1, down).wait_recv()
                kept[z, :, :, :thin] += t_in[z, 1].astype(jnp.float32)

            m_out[...] = kept[z, 1, :, :thin].astype(jnp.bfloat16)
            m_copy.start()

        return carry

    lax.fori_loop(0, nz, second, 0)
    m_copy.wait_recv()
    kept[z, 0, :, :thin] += m_in[...].astype(jnp.float32)
    gathered[me] = kept[z, 0].astype(jnp.bfloat16)

    def block(site):
        return gathered.at[site]

    def slim(ref):
        return ref.at[:, pl.ds(0, thin), :]

    def rest(site):
        return gathered.at[site, :, pl.ds(thin, rows - thin), :]

    def pair(site):
        first_of = pl.multiple_of(site // PAIR * PAIR, PAIR)
        return gathered.at[pl.ds(first_of, PAIR), :, pl.ds(0, thin), :]

    def to_up(site):
        return send(rest(site), rest(site), g_up.at[site // PAIR], g_recv.at[site], up)

    def to_down(site):
        return send(rest(site), rest(site), g_down.at[site // PAIR], g_recv.at[site], down)

    def to_mate(site):
        return send(rest(site), rest(site), g_pair.at[site // PAIR], g_recv.at[site], mate)

    def slim_up(site):
        line = site // PAIR
        return send(pair(site), pair(site), s_up.at[line], s_recv.at[line], up)

    def slim_down(site):
        line = site // PAIR
        return send(pair(site), pair(site), s_down.at[line], s_recv.at[line], down)

    def slim_mate(site):
        return send(slim(block(site)), slim(block(site)), s_pair, s_recv.at[z], mate)

    own = block(me)

    @pl.when(has_up)
    def _():
        to_up(me).start()

    @pl.when(has_down)
    def _():
        to_down(me).start()

    slim_mate(me).start()
    to_mate(me).start()
    meson_copy = pltpu.make_async_copy(own, meson_ref, leave.at[0])
    meson_copy.start()

    slim_mate(mate).wait_recv()

    @pl.when((z == 0) & has_up)
    def _():
        slim_up(me).start()

    @pl.when((z == nz - 1) & has_down)
    def _():
        slim_down(me).start()

    far_copy.wait()

    def gain(value, site):
        lines = pl.ds(pl.multiple_of(site * cols, cols), cols)
        both = value[...].reshape(2 * rows, cols)

        def dot(part):
            whole = jnp.dot(both, field[part, lines, :], preferred_element_type=jnp.float32)
            return whole[:rows], whole[rows:]

        real_real, imag_real = dot(0)
        real_imag, imag_imag = dot(1)
        return (real_real - imag_imag, real_imag + imag_real)

    for part, value in enumerate(gain(own, me)):
        total[part] = value

    def arrive(site):
        for part, value in enumerate(gain(block(site), site)):
            total[part] += value

    def relay(d, carry):
        below = me - d * PAIR
        above = me + d * PAIR

        @pl.when(z >= d)
        def _():
            to_up(below).wait_recv()

            @pl.when(has_up)
            def _():
                to_up(below).start()

            to_mate(below).start()

        @pl.when((z == d) & has_up)
        def _():
            slim_up(me).start()

        @pl.when(z + d < nz)
        def _():
            to_down(above).wait_recv()

            @pl.when(has_down)
            def _():
                to_down(above).start()

            to_mate(above).start()

        @pl.when((z + d == nz - 1) & has_down)
        def _():
            slim_down(me).start()

        return carry

    lax.fori_loop(1, nz, relay, 0)

    def thins(d, carry):
        below = me - d * PAIR
        above = me + d * PAIR

        @pl.when(z >= d)
        def _():
            slim_up(below).wait_recv()

            @pl.when(has_up)
            def _():
                slim_up(below).start()

        @pl.when(z + d < nz)
        def _():
            slim_down(above).wait_recv()

            @pl.when(has_down)
            def _():
                slim_down(above).start()

        @pl.when(z >= d)
        def _():
            arrive(below)

        @pl.when(z + d < nz)
        def _():
            arrive(above)

        return carry

    lax.fori_loop(1, nz, thins, 0)

    def across(d, carry):
        @pl.when(z >= d)
        def _():
            site = mate - d * PAIR
            to_mate(site).wait_recv()
            arrive(site)

        @pl.when((z + d < nz) & (d > 0))
        def _():
            site = mate + d * PAIR
            to_mate(site).wait_recv()
            arrive(site)

        return carry

    lax.fori_loop(0, nz, across, 0)
    copies = [meson_copy]
    for part in range(2):
        staged[part] = total[part].astype(jnp.bfloat16)
        copy = pltpu.make_async_copy(staged.at[part], product_ref.at[part], leave.at[1 + part])
        copy.start()
        copies.append(copy)

    def drain(k, carry):
        x_copy(k).wait_send()

        @pl.when(k != z)
        def _():
            z_copy(k, 0, mate).wait_send()
            t_copy(k, 0, mate).wait_send()

        to_mate(k * PAIR + x).wait_send()

        @pl.when((k <= z) & has_up)
        def _():
            to_up(k * PAIR + x).wait_send()
            slim_up(k * PAIR).wait_send()

        @pl.when((k >= z) & has_down)
        def _():
            to_down(k * PAIR + x).wait_send()
            slim_down(k * PAIR).wait_send()

        return carry

    lax.fori_loop(0, nz, drain, 0)
    slim_mate(me).wait_send()
    m_copy.wait_send()
    for copy in copies:
        copy.wait()


def settle(meson_in, product_in, meson_ref, product_ref, held, in_sem, out_sem):
    parts = meson_in.shape[0]
    pairs = [(meson_in, meson_ref), (product_in, product_ref)]
    into, out = [], []
    for which, (src, dst) in enumerate(pairs):
        for part in range(parts):
            slot = which * parts + part
            into.append(pltpu.make_async_copy(src.at[part], held.at[slot], in_sem.at[slot]))
            out.append(pltpu.make_async_copy(held.at[slot], dst.at[part], out_sem.at[slot]))
    for copy in into:
        copy.start()
    for arrived, copy in zip(into, out):
        arrived.wait()
        copy.start()
    for copy in out:
        copy.wait()


def body(left_modes, right_modes, momenta, far_fields):
    times = lax.axis_size("tm")
    groups = lax.axis_size("site")
    nz = groups // PAIR
    rows, width = left_modes.shape[2:]
    modes, cols = far_fields.shape[2:]
    factor = (2.0 * width * groups) ** (-0.5)
    chunk = (2, rows, cols)
    thin = thin_rows(rows)
    large = (2, rows - thin, cols)
    small = (2, thin, cols)
    dma = pltpu.SemaphoreType.DMA
    meson, product = pl.pallas_call(
        functools.partial(kernel, times, groups, factor),
        out_shape=[jax.ShapeDtypeStruct(chunk, jnp.bfloat16)] * 2,
        in_specs=[
            pl.BlockSpec(memory_space=pl.ANY),
            pl.BlockSpec(memory_space=pl.ANY),
            pl.BlockSpec(memory_space=pltpu.SMEM),
            pl.BlockSpec(memory_space=pl.ANY),
        ],
        out_specs=[pl.BlockSpec(memory_space=pl.ANY)] * 2,
        scratch_shapes=[
            pltpu.VMEM((2 * rows, 2 * width), jnp.bfloat16),
            pltpu.VMEM((2, modes, cols), jnp.bfloat16),
            pltpu.VMEM((nz,) + large, jnp.bfloat16),
            pltpu.VMEM((nz,) + large, jnp.bfloat16),
            pltpu.VMEM((nz,) + large, jnp.bfloat16),
            pltpu.VMEM((nz, 2) + large, jnp.bfloat16),
            pltpu.VMEM((groups,) + chunk, jnp.bfloat16),
            pltpu.VMEM(chunk, jnp.float32),
            dma(()),
            dma(()),
            dma((nz,)),
            dma((nz,)),
            dma((nz,)),
            dma((nz, 2)),
            dma((groups,)),
            dma((nz,)),
            dma((nz,)),
            dma((nz,)),
            dma((nz,)),
            dma((nz,)),
            dma((nz,)),
            dma(()),
            pltpu.VMEM((2, width, rows), jnp.bfloat16),
            pltpu.VMEM((groups, 2, width, cols), jnp.bfloat16),
            dma(()),
            dma((groups,)),
            pltpu.VMEM((nz, PAIR) + chunk, jnp.float32),
            pltpu.VMEM((nz, PAIR) + small, jnp.bfloat16),
            pltpu.VMEM((nz, 2, PAIR) + small, jnp.bfloat16),
            dma((nz,)),
            dma((nz, 2)),
            pltpu.VMEM(small, jnp.bfloat16),
            pltpu.VMEM(small, jnp.bfloat16),
            dma((2,)),
            pltpu.VMEM(chunk, jnp.bfloat16),
            dma((3,)),
        ],
        compiler_params=pltpu.CompilerParams(
            collective_id=0, has_side_effects=True, vmem_limit_bytes=60 * 2**20
        ),
    )(
        jnp.swapaxes(left_modes[0], 1, 2),
        jnp.swapaxes(right_modes[0], 1, 2),
        momenta,
        far_fields[0],
    )
    meson, product = pl.pallas_call(
        settle,
        out_shape=[jax.ShapeDtypeStruct(chunk, jnp.bfloat16)] * 2,
        in_specs=[pl.BlockSpec(memory_space=pl.ANY)] * 2,
        out_specs=[pl.BlockSpec(memory_space=pl.ANY)] * 2,
        scratch_shapes=[pltpu.VMEM((4, rows, cols), jnp.bfloat16), dma((4,)), dma((4,))],
        compiler_params=pltpu.CompilerParams(vmem_limit_bytes=60 * 2**20),
    )(meson, product)
    return (meson[None], product[None])


def solution(mesh):
    return jax.shard_map(
        body,
        mesh=mesh,
        in_specs=(
            P("tm", None, None, "site"),
            P("tm", None, None, "site"),
            P("tm", None),
            P("tm", None, None, "site"),
        ),
        out_specs=(P("tm", None, None, "site"), P("tm", None, None, "site")),
        check_vma=False,
    )
```

```python
import functools
import math

import jax
import jax.numpy as jnp
from jax import lax
from jax.experimental import pallas as pl
from jax.experimental.pallas import tpu as pltpu
from jax.sharding import PartitionSpec as P

SC = 12
EXTENT = 96
DT = 3
PAIR = 2
MESH = pl.DeviceIdType.MESH


def block_coords(sites):
    coords = []
    for axis in range(3):
        coord = jnp.zeros_like(sites)
        for level in range(7):
            coord = coord + ((sites >> (3 * level + axis)) & 1) * 2**level
        coords.append(coord)
    return coords


def thin_rows(rows):
    return max(16, rows // 6 // 16 * 16)


def order(k, z, nz):
    short = jnp.minimum(z, nz - 1 - z)
    lone = nz - 1 - 2 * short
    toward = jnp.where(z < nz - 1 - z, 1, -1)
    rest = k - lone
    far = z + toward * (nz - 1 - short - k)
    near = z + (short - rest // 2) * (1 - 2 * (rest % 2))
    return jnp.where(k == nz - 1, z, jnp.where(k < lone, far, near))


def kernel(
    times,
    groups,
    factor,
    left_ref,
    right_ref,
    momenta_ref,
    far_ref,
    meson_ref,
    product_ref,
    phased,
    field,
    x_out,
    x_in,
    z_out,
    z_in,
    gathered,
    total,
    far_send,
    far_recv,
    xo_sem,
    xi_sem,
    zo_sem,
    zi_sem,
    g_recv,
    g_up,
    g_down,
    g_pair,
    s_recv,
    s_up,
    s_down,
    s_pair,
    left_in,
    right_in,
    left_sem,
    right_sem,
    kept,
    t_out,
    t_in,
    to_sem,
    ti_sem,
    m_out,
    m_in,
    m_sem,
    staged,
    leave,
):
    nz = groups // PAIR
    rows, cols = meson_ref.shape[1:]
    width = left_ref.shape[1]
    thin = thin_rows(rows)
    tm = lax.axis_index("tm")
    me = lax.axis_index("site")
    z = me // PAIR
    x = me % PAIR
    mate = z * PAIR + (1 - x)
    up = me + PAIR
    down = me - PAIR
    has_up = z < nz - 1
    has_down = z > 0
    target = lax.rem(tm + times - DT % times, times)
    source = lax.rem(tm + DT, times)

    left_copy = pltpu.make_async_copy(left_ref, left_in, left_sem)
    left_copy.start()

    def right_copy(site):
        lanes = pl.ds(pl.multiple_of(site * cols, cols), cols)
        return pltpu.make_async_copy(right_ref.at[:, :, lanes], right_in.at[site], right_sem.at[site])

    def load(k, carry):
        dest = order(k, z, nz)
        right_copy(dest * PAIR + (1 - x)).start()
        right_copy(dest * PAIR + x).start()
        return carry

    lax.fori_loop(0, nz, load, 0)

    barrier = pltpu.get_barrier_semaphore()
    pl.semaphore_signal(barrier, inc=1, device_id=(target, me), device_id_type=MESH)
    pl.semaphore_signal(barrier, inc=1, device_id=(source, me), device_id_type=MESH)
    pl.semaphore_signal(barrier, inc=1, device_id=(tm, mate), device_id_type=MESH)

    @pl.when(has_up)
    def _():
        pl.semaphore_signal(barrier, inc=1, device_id=(tm, up), device_id_type=MESH)

    @pl.when(has_down)
    def _():
        pl.semaphore_signal(barrier, inc=1, device_id=(tm, down), device_id_type=MESH)

    def send(src, dst, send_sem, recv_sem, site):
        return pltpu.make_async_remote_copy(
            src_ref=src,
            dst_ref=dst,
            send_sem=send_sem,
            recv_sem=recv_sem,
            device_id=(tm, site),
            device_id_type=MESH,
        )

    column = lax.broadcasted_iota(jnp.int32, (width, 128), 0)
    inside = jnp.floor((column.astype(jnp.float32) + 0.5) / SC).astype(jnp.int32)
    sites = me * (width // SC) + inside
    coords = block_coords(sites)
    wave = sum(momenta_ref[0, axis] * coords[axis] for axis in range(3)).astype(jnp.float32)
    wave = wave - EXTENT * jnp.floor((wave + 0.5) / EXTENT)
    angles = 2.0 * math.pi / EXTENT * wave
    cosine = jnp.cos(angles)[:, 0:1]
    sine = jnp.sin(angles)[:, 0:1]
    left_copy.wait()
    real = left_in[0].astype(jnp.float32)
    imag = left_in[1].astype(jnp.float32)
    phased_real = factor * (real * cosine + imag * sine)
    phased_imag = factor * (real * sine - imag * cosine)
    for_real = jnp.concatenate([phased_real, -phased_imag], axis=0)
    for_imag = jnp.concatenate([phased_imag, phased_real], axis=0)
    phased[0:rows, :] = for_real.T.astype(jnp.bfloat16)
    phased[rows : 2 * rows, :] = for_imag.T.astype(jnp.bfloat16)

    pl.semaphore_wait(barrier, 3 + has_up.astype(jnp.int32) + has_down.astype(jnp.int32))

    far_copy = pltpu.make_async_remote_copy(
        src_ref=far_ref,
        dst_ref=field,
        send_sem=far_send,
        recv_sem=far_recv,
        device_id=(target, me),
        device_id_type=MESH,
    )
    far_copy.start()

    def partial(site):
        right_copy(site).wait()
        right = right_in[site].reshape(2 * width, cols)
        both = jnp.dot(phased[...], right, preferred_element_type=jnp.float32)
        return both.reshape(2, rows, cols)

    def x_copy(dest, part):
        return send(
            x_out.at[dest, part],
            x_in.at[dest, part],
            xo_sem.at[dest, part],
            xi_sem.at[dest, part],
            mate,
        )

    def z_copy(dest, part, side, site):
        return send(
            z_out.at[dest, part],
            z_in.at[dest, side, part],
            zo_sem.at[dest, part],
            zi_sem.at[dest, side, part],
            site,
        )

    def t_copy(dest, side, site):
        return send(
            t_out.at[dest], t_in.at[dest, side], to_sem.at[dest], ti_sem.at[dest, side], site
        )

    m_copy = send(m_out, m_in, m_sem.at[0], m_sem.at[1], mate)

    def first(k, carry):
        dest = order(k, z, nz)
        theirs = partial(dest * PAIR + (1 - x))
        for part in range(2):
            x_out[dest, part] = theirs[part, thin:].astype(jnp.bfloat16)
            x_copy(dest, part).start()
        kept[dest, 1, :, :thin] = theirs[:, :thin]
        kept[dest, 0] = partial(dest * PAIR + x)

        @pl.when((dest > z) & has_down)
        def _():
            t_copy(dest, 0, up).wait_recv()
            kept[dest, :, :, :thin] += t_in[dest, 0].astype(jnp.float32)

        @pl.when((dest < z) & has_up)
        def _():
            t_copy(dest, 1, down).wait_recv()
            kept[dest, :, :, :thin] += t_in[dest, 1].astype(jnp.float32)

        @pl.when(dest > z)
        def _():
            t_out[dest] = kept[dest, :, :, :thin].astype(jnp.bfloat16)
            t_copy(dest, 0, up).start()

        @pl.when(dest < z)
        def _():
            t_out[dest] = kept[dest, :, :, :thin].astype(jnp.bfloat16)
            t_copy(dest, 1, down).start()

        return carry

    lax.fori_loop(0, nz, first, 0)

    def block(site):
        return gathered.at[site]

    def slim(ref):
        return ref.at[:, pl.ds(0, thin), :]

    def rest(site, part):
        return gathered.at[site, part, pl.ds(thin, rows - thin), :]

    def pair(site):
        first_of = pl.multiple_of(site // PAIR * PAIR, PAIR)
        return gathered.at[pl.ds(first_of, PAIR), :, pl.ds(0, thin), :]

    def rest_copy(site, part, sem, to):
        src = rest(site, part)
        return send(src, src, sem.at[site // PAIR, part], g_recv.at[site, part], to)

    def to_up(site, part):
        return rest_copy(site, part, g_up, up)

    def to_down(site, part):
        return rest_copy(site, part, g_down, down)

    def to_mate(site, part):
        return rest_copy(site, part, g_pair, mate)

    def second(k, carry):
        dest = order(k, z, nz)
        for part in range(2):
            x_copy(dest, part).wait_recv()
            kept[dest, 0, part, thin:] += x_in[dest, part].astype(jnp.float32)

            @pl.when((dest >= z) & has_down)
            def _():
                z_copy(dest, part, 0, up).wait_recv()
                kept[dest, 0, part, thin:] += z_in[dest, 0, part].astype(jnp.float32)

            @pl.when((dest <= z) & has_up)
            def _():
                z_copy(dest, part, 1, down).wait_recv()
                kept[dest, 0, part, thin:] += z_in[dest, 1, part].astype(jnp.float32)

            @pl.when(dest > z)
            def _():
                z_out[dest, part] = kept[dest, 0, part, thin:].astype(jnp.bfloat16)
                z_copy(dest, part, 0, up).start()

            @pl.when(dest < z)
            def _():
                z_out[dest, part] = kept[dest, 0, part, thin:].astype(jnp.bfloat16)
                z_copy(dest, part, 1, down).start()

            @pl.when(dest == z)
            def _():
                gathered[me, part, thin:] = kept[z, 0, part, thin:].astype(jnp.bfloat16)

                @pl.when(has_up)
                def _():
                    to_up(me, part).start()

                @pl.when(has_down)
                def _():
                    to_down(me, part).start()

                to_mate(me, part).start()

        @pl.when(k == 0)
        def _():
            @pl.when(has_down)
            def _():
                t_copy(z, 0, up).wait_recv()
                kept[z, :, :, :thin] += t_in[z, 0].astype(jnp.float32)

            @pl.when(has_up)
            def _():
                t_copy(z, 1, down).wait_recv()
                kept[z, :, :, :thin] += t_in[z, 1].astype(jnp.float32)

            m_out[...] = kept[z, 1, :, :thin].astype(jnp.bfloat16)
            m_copy.start()

        return carry

    lax.fori_loop(0, nz, second, 0)
    m_copy.wait_recv()
    kept[z, 0, :, :thin] += m_in[...].astype(jnp.float32)
    gathered[me, :, :thin] = kept[z, 0, :, :thin].astype(jnp.bfloat16)

    def slim_up(site):
        line = site // PAIR
        return send(pair(site), pair(site), s_up.at[line], s_recv.at[line], up)

    def slim_down(site):
        line = site // PAIR
        return send(pair(site), pair(site), s_down.at[line], s_recv.at[line], down)

    def slim_mate(site):
        return send(slim(block(site)), slim(block(site)), s_pair, s_recv.at[z], mate)

    own = block(me)
    slim_mate(me).start()
    meson_copy = pltpu.make_async_copy(own, meson_ref, leave.at[0])
    meson_copy.start()

    slim_mate(mate).wait_recv()

    @pl.when((z == 0) & has_up)
    def _():
        slim_up(me).start()

    @pl.when((z == nz - 1) & has_down)
    def _():
        slim_down(me).start()

    far_copy.wait()

    def gain(value, site):
        lines = pl.ds(pl.multiple_of(site * cols, cols), cols)
        both = value[...].reshape(2 * rows, cols)

        def dot(part):
            whole = jnp.dot(both, field[part, lines, :], preferred_element_type=jnp.float32)
            return whole[:rows], whole[rows:]

        real_real, imag_real = dot(0)
        real_imag, imag_imag = dot(1)
        return (real_real - imag_imag, real_imag + imag_real)

    for part, value in enumerate(gain(own, me)):
        total[part] = value

    def arrive(site):
        for part, value in enumerate(gain(block(site), site)):
            total[part] += value

    def relay(d, carry):
        below = me - d * PAIR
        above = me + d * PAIR

        for part in range(2):

            @pl.when(z >= d)
            def _():
                to_up(below, part).wait_recv()

                @pl.when(has_up)
                def _():
                    to_up(below, part).start()

                to_mate(below, part).start()

            @pl.when(z + d < nz)
            def _():
                to_down(above, part).wait_recv()

                @pl.when(has_down)
                def _():
                    to_down(above, part).start()

                to_mate(above, part).start()

        @pl.when((z == d) & has_up)
        def _():
            slim_up(me).start()

        @pl.when((z + d == nz - 1) & has_down)
        def _():
            slim_down(me).start()

        return carry

    lax.fori_loop(1, nz, relay, 0)

    def thins(d, carry):
        below = me - d * PAIR
        above = me + d * PAIR

        @pl.when(z >= d)
        def _():
            slim_up(below).wait_recv()

            @pl.when(has_up)
            def _():
                slim_up(below).start()

        @pl.when(z + d < nz)
        def _():
            slim_down(above).wait_recv()

            @pl.when(has_down)
            def _():
                slim_down(above).start()

        @pl.when(z >= d)
        def _():
            arrive(below)

        @pl.when(z + d < nz)
        def _():
            arrive(above)

        return carry

    lax.fori_loop(1, nz, thins, 0)

    def across(d, carry):
        @pl.when(z >= d)
        def _():
            site = mate - d * PAIR
            to_mate(site, 0).wait_recv()
            to_mate(site, 1).wait_recv()
            arrive(site)

        @pl.when((z + d < nz) & (d > 0))
        def _():
            site = mate + d * PAIR
            to_mate(site, 0).wait_recv()
            to_mate(site, 1).wait_recv()
            arrive(site)

        return carry

    lax.fori_loop(0, nz, across, 0)
    copies = [meson_copy]
    for part in range(2):
        staged[part] = total[part].astype(jnp.bfloat16)
        copy = pltpu.make_async_copy(staged.at[part], product_ref.at[part], leave.at[1 + part])
        copy.start()
        copies.append(copy)

    def drain(k, carry):
        for part in range(2):
            x_copy(k, part).wait_send()
            to_mate(k * PAIR + x, part).wait_send()

            @pl.when(k != z)
            def _():
                z_copy(k, part, 0, mate).wait_send()

            @pl.when((k <= z) & has_up)
            def _():
                to_up(k * PAIR + x, part).wait_send()

            @pl.when((k >= z) & has_down)
            def _():
                to_down(k * PAIR + x, part).wait_send()

        @pl.when(k != z)
        def _():
            t_copy(k, 0, mate).wait_send()

        @pl.when((k <= z) & has_up)
        def _():
            slim_up(k * PAIR).wait_send()

        @pl.when((k >= z) & has_down)
        def _():
            slim_down(k * PAIR).wait_send()

        return carry

    lax.fori_loop(0, nz, drain, 0)
    slim_mate(me).wait_send()
    m_copy.wait_send()
    for copy in copies:
        copy.wait()


def settle(meson_in, product_in, meson_ref, product_ref, held, in_sem, out_sem):
    parts = meson_in.shape[0]
    pairs = [(meson_in, meson_ref), (product_in, product_ref)]
    into, out = [], []
    for which, (src, dst) in enumerate(pairs):
        for part in range(parts):
            slot = which * parts + part
            into.append(pltpu.make_async_copy(src.at[part], held.at[slot], in_sem.at[slot]))
            out.append(pltpu.make_async_copy(held.at[slot], dst.at[part], out_sem.at[slot]))
    for copy in into:
        copy.start()
    for arrived, copy in zip(into, out):
        arrived.wait()
        copy.start()
    for copy in out:
        copy.wait()


def body(left_modes, right_modes, momenta, far_fields):
    times = lax.axis_size("tm")
    groups = lax.axis_size("site")
    nz = groups // PAIR
    rows, width = left_modes.shape[2:]
    modes, cols = far_fields.shape[2:]
    factor = (2.0 * width * groups) ** (-0.5)
    chunk = (2, rows, cols)
    thin = thin_rows(rows)
    large = (2, rows - thin, cols)
    small = (2, thin, cols)
    dma = pltpu.SemaphoreType.DMA
    meson, product = pl.pallas_call(
        functools.partial(kernel, times, groups, factor),
        out_shape=[jax.ShapeDtypeStruct(chunk, jnp.bfloat16)] * 2,
        in_specs=[
            pl.BlockSpec(memory_space=pl.ANY),
            pl.BlockSpec(memory_space=pl.ANY),
            pl.BlockSpec(memory_space=pltpu.SMEM),
            pl.BlockSpec(memory_space=pl.ANY),
        ],
        out_specs=[pl.BlockSpec(memory_space=pl.ANY)] * 2,
        scratch_shapes=[
            pltpu.VMEM((2 * rows, 2 * width), jnp.bfloat16),
            pltpu.VMEM((2, modes, cols), jnp.bfloat16),
            pltpu.VMEM((nz,) + large, jnp.bfloat16),
            pltpu.VMEM((nz,) + large, jnp.bfloat16),
            pltpu.VMEM((nz,) + large, jnp.bfloat16),
            pltpu.VMEM((nz, 2) + large, jnp.bfloat16),
            pltpu.VMEM((groups,) + chunk, jnp.bfloat16),
            pltpu.VMEM(chunk, jnp.float32),
            dma(()),
            dma(()),
            dma((nz, 2)),
            dma((nz, 2)),
            dma((nz, 2)),
            dma((nz, 2, 2)),
            dma((groups, 2)),
            dma((nz, 2)),
            dma((nz, 2)),
            dma((nz, 2)),
            dma((nz,)),
            dma((nz,)),
            dma((nz,)),
            dma(()),
            pltpu.VMEM((2, width, rows), jnp.bfloat16),
            pltpu.VMEM((groups, 2, width, cols), jnp.bfloat16),
            dma(()),
            dma((groups,)),
            pltpu.VMEM((nz, PAIR) + chunk, jnp.float32),
            pltpu.VMEM((nz, PAIR) + small, jnp.bfloat16),
            pltpu.VMEM((nz, 2, PAIR) + small, jnp.bfloat16),
            dma((nz,)),
            dma((nz, 2)),
            pltpu.VMEM(small, jnp.bfloat16),
            pltpu.VMEM(small, jnp.bfloat16),
            dma((2,)),
            pltpu.VMEM(chunk, jnp.bfloat16),
            dma((3,)),
        ],
        compiler_params=pltpu.CompilerParams(
            collective_id=0, has_side_effects=True, vmem_limit_bytes=60 * 2**20
        ),
    )(
        jnp.swapaxes(left_modes[0], 1, 2),
        jnp.swapaxes(right_modes[0], 1, 2),
        momenta,
        far_fields[0],
    )
    meson, product = pl.pallas_call(
        settle,
        out_shape=[jax.ShapeDtypeStruct(chunk, jnp.bfloat16)] * 2,
        in_specs=[pl.BlockSpec(memory_space=pl.ANY)] * 2,
        out_specs=[pl.BlockSpec(memory_space=pl.ANY)] * 2,
        scratch_shapes=[pltpu.VMEM((4, rows, cols), jnp.bfloat16), dma((4,)), dma((4,))],
        compiler_params=pltpu.CompilerParams(vmem_limit_bytes=60 * 2**20),
    )(meson, product)
    return (meson[None], product[None])


def solution(mesh):
    return jax.shard_map(
        body,
        mesh=mesh,
        in_specs=(
            P("tm", None, None, "site"),
            P("tm", None, None, "site"),
            P("tm", None),
            P("tm", None, None, "site"),
        ),
        out_specs=(P("tm", None, None, "site"), P("tm", None, None, "site")),
        check_vma=False,
    )
```

```python
import functools
import math

import jax
import jax.numpy as jnp
from jax import lax
from jax.experimental import pallas as pl
from jax.experimental.pallas import tpu as pltpu
from jax.sharding import PartitionSpec as P

SC = 12
EXTENT = 96
DT = 3
PAIR = 2
MESH = pl.DeviceIdType.MESH


def block_coords(sites):
    coords = []
    for axis in range(3):
        coord = jnp.zeros_like(sites)
        for level in range(7):
            coord = coord + ((sites >> (3 * level + axis)) & 1) * 2**level
        coords.append(coord)
    return coords


def thin_rows(rows):
    return max(16, rows * 3 // 16 // 16 * 16)


def order(k, z, nz):
    short = jnp.minimum(z, nz - 1 - z)
    lone = nz - 1 - 2 * short
    toward = jnp.where(z < nz - 1 - z, 1, -1)
    rest = k - lone
    far = z + toward * (nz - 1 - short - k)
    near = z + (short - rest // 2) * (1 - 2 * (rest % 2))
    return jnp.where(k == nz - 1, z, jnp.where(k < lone, far, near))


def kernel(
    times,
    groups,
    factor,
    left_ref,
    right_ref,
    momenta_ref,
    far_ref,
    meson_ref,
    product_ref,
    phased,
    field,
    x_out,
    x_in,
    z_out,
    z_in,
    gathered,
    total,
    far_send,
    far_recv,
    xo_sem,
    xi_sem,
    zo_sem,
    zi_sem,
    g_recv,
    g_up,
    g_down,
    g_pair,
    s_recv,
    s_up,
    s_down,
    s_pair,
    left_in,
    right_in,
    left_sem,
    right_sem,
    kept,
    t_out,
    t_in,
    to_sem,
    ti_sem,
    m_out,
    m_in,
    m_sem,
    staged,
    leave,
):
    nz = groups // PAIR
    rows, cols = meson_ref.shape[1:]
    width = left_ref.shape[1]
    thin = thin_rows(rows)
    tm = lax.axis_index("tm")
    me = lax.axis_index("site")
    z = me // PAIR
    x = me % PAIR
    mate = z * PAIR + (1 - x)
    up = me + PAIR
    down = me - PAIR
    has_up = z < nz - 1
    has_down = z > 0
    target = lax.rem(tm + times - DT % times, times)
    source = lax.rem(tm + DT, times)

    left_copy = pltpu.make_async_copy(left_ref, left_in, left_sem)
    left_copy.start()

    def right_copy(site):
        lanes = pl.ds(pl.multiple_of(site * cols, cols), cols)
        return pltpu.make_async_copy(right_ref.at[:, :, lanes], right_in.at[site], right_sem.at[site])

    def load(k, carry):
        dest = order(k, z, nz)
        right_copy(dest * PAIR + (1 - x)).start()
        right_copy(dest * PAIR + x).start()
        return carry

    lax.fori_loop(0, nz, load, 0)

    barrier = pltpu.get_barrier_semaphore()
    pl.semaphore_signal(barrier, inc=1, device_id=(target, me), device_id_type=MESH)
    pl.semaphore_signal(barrier, inc=1, device_id=(source, me), device_id_type=MESH)
    pl.semaphore_signal(barrier, inc=1, device_id=(tm, mate), device_id_type=MESH)

    @pl.when(has_up)
    def _():
        pl.semaphore_signal(barrier, inc=1, device_id=(tm, up), device_id_type=MESH)

    @pl.when(has_down)
    def _():
        pl.semaphore_signal(barrier, inc=1, device_id=(tm, down), device_id_type=MESH)

    def send(src, dst, send_sem, recv_sem, site):
        return pltpu.make_async_remote_copy(
            src_ref=src,
            dst_ref=dst,
            send_sem=send_sem,
            recv_sem=recv_sem,
            device_id=(tm, site),
            device_id_type=MESH,
        )

    column = lax.broadcasted_iota(jnp.int32, (width, 128), 0)
    inside = jnp.floor((column.astype(jnp.float32) + 0.5) / SC).astype(jnp.int32)
    sites = me * (width // SC) + inside
    coords = block_coords(sites)
    wave = sum(momenta_ref[0, axis] * coords[axis] for axis in range(3)).astype(jnp.float32)
    wave = wave - EXTENT * jnp.floor((wave + 0.5) / EXTENT)
    angles = 2.0 * math.pi / EXTENT * wave
    cosine = jnp.cos(angles)[:, 0:1]
    sine = jnp.sin(angles)[:, 0:1]
    left_copy.wait()
    real = left_in[0].astype(jnp.float32)
    imag = left_in[1].astype(jnp.float32)
    phased_real = factor * (real * cosine + imag * sine)
    phased_imag = factor * (real * sine - imag * cosine)
    for_real = jnp.concatenate([phased_real, -phased_imag], axis=0)
    for_imag = jnp.concatenate([phased_imag, phased_real], axis=0)
    phased[0:rows, :] = for_real.T.astype(jnp.bfloat16)
    phased[rows : 2 * rows, :] = for_imag.T.astype(jnp.bfloat16)

    pl.semaphore_wait(barrier, 3 + has_up.astype(jnp.int32) + has_down.astype(jnp.int32))

    far_copy = pltpu.make_async_remote_copy(
        src_ref=far_ref,
        dst_ref=field,
        send_sem=far_send,
        recv_sem=far_recv,
        device_id=(target, me),
        device_id_type=MESH,
    )
    far_copy.start()

    def partial(site):
        right_copy(site).wait()
        right = right_in[site].reshape(2 * width, cols)
        both = jnp.dot(phased[...], right, preferred_element_type=jnp.float32)
        return both.reshape(2, rows, cols)

    def x_copy(dest, part):
        return send(
            x_out.at[dest, part],
            x_in.at[dest, part],
            xo_sem.at[dest, part],
            xi_sem.at[dest, part],
            mate,
        )

    def z_copy(dest, part, side, site):
        return send(
            z_out.at[dest, part],
            z_in.at[dest, side, part],
            zo_sem.at[dest, part],
            zi_sem.at[dest, side, part],
            site,
        )

    def t_copy(dest, side, site):
        return send(
            t_out.at[dest], t_in.at[dest, side], to_sem.at[dest], ti_sem.at[dest, side], site
        )

    m_copy = send(m_out, m_in, m_sem.at[0], m_sem.at[1], mate)

    def first(k, carry):
        dest = order(k, z, nz)
        theirs = partial(dest * PAIR + (1 - x))
        for part in range(2):
            x_out[dest, part] = theirs[part, thin:].astype(jnp.bfloat16)
            x_copy(dest, part).start()
        kept[dest, 1, :, :thin] = theirs[:, :thin]
        kept[dest, 0] = partial(dest * PAIR + x)

        @pl.when((dest > z) & has_down)
        def _():
            t_copy(dest, 0, up).wait_recv()
            kept[dest, :, :, :thin] += t_in[dest, 0].astype(jnp.float32)

        @pl.when((dest < z) & has_up)
        def _():
            t_copy(dest, 1, down).wait_recv()
            kept[dest, :, :, :thin] += t_in[dest, 1].astype(jnp.float32)

        @pl.when(dest > z)
        def _():
            t_out[dest] = kept[dest, :, :, :thin].astype(jnp.bfloat16)
            t_copy(dest, 0, up).start()

        @pl.when(dest < z)
        def _():
            t_out[dest] = kept[dest, :, :, :thin].astype(jnp.bfloat16)
            t_copy(dest, 1, down).start()

        return carry

    lax.fori_loop(0, nz, first, 0)

    def block(site):
        return gathered.at[site]

    def slim(ref):
        return ref.at[:, pl.ds(0, thin), :]

    def rest(site, part):
        return gathered.at[site, part, pl.ds(thin, rows - thin), :]

    def pair(site):
        first_of = pl.multiple_of(site // PAIR * PAIR, PAIR)
        return gathered.at[pl.ds(first_of, PAIR), :, pl.ds(0, thin), :]

    def rest_copy(site, part, sem, to):
        src = rest(site, part)
        return send(src, src, sem.at[site // PAIR, part], g_recv.at[site, part], to)

    def to_up(site, part):
        return rest_copy(site, part, g_up, up)

    def to_down(site, part):
        return rest_copy(site, part, g_down, down)

    def to_mate(site, part):
        return rest_copy(site, part, g_pair, mate)

    def second(k, carry):
        dest = order(k, z, nz)
        for part in range(2):
            x_copy(dest, part).wait_recv()
            kept[dest, 0, part, thin:] += x_in[dest, part].astype(jnp.float32)

            @pl.when((dest >= z) & has_down)
            def _():
                z_copy(dest, part, 0, up).wait_recv()
                kept[dest, 0, part, thin:] += z_in[dest, 0, part].astype(jnp.float32)

            @pl.when((dest <= z) & has_up)
            def _():
                z_copy(dest, part, 1, down).wait_recv()
                kept[dest, 0, part, thin:] += z_in[dest, 1, part].astype(jnp.float32)

            @pl.when(dest > z)
            def _():
                z_out[dest, part] = kept[dest, 0, part, thin:].astype(jnp.bfloat16)
                z_copy(dest, part, 0, up).start()

            @pl.when(dest < z)
            def _():
                z_out[dest, part] = kept[dest, 0, part, thin:].astype(jnp.bfloat16)
                z_copy(dest, part, 1, down).start()

            @pl.when(dest == z)
            def _():
                gathered[me, part, thin:] = kept[z, 0, part, thin:].astype(jnp.bfloat16)

                @pl.when(has_up)
                def _():
                    to_up(me, part).start()

                @pl.when(has_down)
                def _():
                    to_down(me, part).start()

                to_mate(me, part).start()

        @pl.when(k == 0)
        def _():
            @pl.when(has_down)
            def _():
                t_copy(z, 0, up).wait_recv()
                kept[z, :, :, :thin] += t_in[z, 0].astype(jnp.float32)

            @pl.when(has_up)
            def _():
                t_copy(z, 1, down).wait_recv()
                kept[z, :, :, :thin] += t_in[z, 1].astype(jnp.float32)

            m_out[...] = kept[z, 1, :, :thin].astype(jnp.bfloat16)
            m_copy.start()

        return carry

    lax.fori_loop(0, nz, second, 0)
    m_copy.wait_recv()
    kept[z, 0, :, :thin] += m_in[...].astype(jnp.float32)
    gathered[me, :, :thin] = kept[z, 0, :, :thin].astype(jnp.bfloat16)

    def slim_up(site):
        line = site // PAIR
        return send(pair(site), pair(site), s_up.at[line], s_recv.at[line], up)

    def slim_down(site):
        line = site // PAIR
        return send(pair(site), pair(site), s_down.at[line], s_recv.at[line], down)

    def slim_mate(site):
        return send(slim(block(site)), slim(block(site)), s_pair, s_recv.at[z], mate)

    own = block(me)
    slim_mate(me).start()
    meson_copy = pltpu.make_async_copy(own, meson_ref, leave.at[0])
    meson_copy.start()

    slim_mate(mate).wait_recv()

    @pl.when((z == 0) & has_up)
    def _():
        slim_up(me).start()

    @pl.when((z == nz - 1) & has_down)
    def _():
        slim_down(me).start()

    far_copy.wait()

    def gain(value, site):
        lines = pl.ds(pl.multiple_of(site * cols, cols), cols)
        both = value[...].reshape(2 * rows, cols)

        def dot(part):
            whole = jnp.dot(both, field[part, lines, :], preferred_element_type=jnp.float32)
            return whole[:rows], whole[rows:]

        real_real, imag_real = dot(0)
        real_imag, imag_imag = dot(1)
        return (real_real - imag_imag, real_imag + imag_real)

    for part, value in enumerate(gain(own, me)):
        total[part] = value

    def arrive(site):
        for part, value in enumerate(gain(block(site), site)):
            total[part] += value

    def relay(d, carry):
        below = me - d * PAIR
        above = me + d * PAIR

        for part in range(2):

            @pl.when(z >= d)
            def _():
                to_up(below, part).wait_recv()

                @pl.when(has_up)
                def _():
                    to_up(below, part).start()

                to_mate(below, part).start()

            @pl.when(z + d < nz)
            def _():
                to_down(above, part).wait_recv()

                @pl.when(has_down)
                def _():
                    to_down(above, part).start()

                to_mate(above, part).start()

        @pl.when((z == d) & has_up)
        def _():
            slim_up(me).start()

        @pl.when((z + d == nz - 1) & has_down)
        def _():
            slim_down(me).start()

        return carry

    lax.fori_loop(1, nz, relay, 0)

    def thins(d, carry):
        below = me - d * PAIR
        above = me + d * PAIR

        @pl.when(z >= d)
        def _():
            slim_up(below).wait_recv()

            @pl.when(has_up)
            def _():
                slim_up(below).start()

        @pl.when(z + d < nz)
        def _():
            slim_down(above).wait_recv()

            @pl.when(has_down)
            def _():
                slim_down(above).start()

        @pl.when(z >= d)
        def _():
            arrive(below)

        @pl.when(z + d < nz)
        def _():
            arrive(above)

        return carry

    lax.fori_loop(1, nz, thins, 0)

    def across(d, carry):
        @pl.when(z >= d)
        def _():
            site = mate - d * PAIR
            to_mate(site, 0).wait_recv()
            to_mate(site, 1).wait_recv()
            arrive(site)

        @pl.when((z + d < nz) & (d > 0))
        def _():
            site = mate + d * PAIR
            to_mate(site, 0).wait_recv()
            to_mate(site, 1).wait_recv()
            arrive(site)

        return carry

    lax.fori_loop(0, nz, across, 0)
    copies = [meson_copy]
    for part in range(2):
        staged[part] = total[part].astype(jnp.bfloat16)
        copy = pltpu.make_async_copy(staged.at[part], product_ref.at[part], leave.at[1 + part])
        copy.start()
        copies.append(copy)

    def drain(k, carry):
        for part in range(2):
            x_copy(k, part).wait_send()
            to_mate(k * PAIR + x, part).wait_send()

            @pl.when(k != z)
            def _():
                z_copy(k, part, 0, mate).wait_send()

            @pl.when((k <= z) & has_up)
            def _():
                to_up(k * PAIR + x, part).wait_send()

            @pl.when((k >= z) & has_down)
            def _():
                to_down(k * PAIR + x, part).wait_send()

        @pl.when(k != z)
        def _():
            t_copy(k, 0, mate).wait_send()

        @pl.when((k <= z) & has_up)
        def _():
            slim_up(k * PAIR).wait_send()

        @pl.when((k >= z) & has_down)
        def _():
            slim_down(k * PAIR).wait_send()

        return carry

    lax.fori_loop(0, nz, drain, 0)
    slim_mate(me).wait_send()
    m_copy.wait_send()
    for copy in copies:
        copy.wait()


def settle(meson_in, product_in, meson_ref, product_ref, held, in_sem, out_sem):
    parts = meson_in.shape[0]
    pairs = [(meson_in, meson_ref), (product_in, product_ref)]
    into, out = [], []
    for which, (src, dst) in enumerate(pairs):
        for part in range(parts):
            slot = which * parts + part
            into.append(pltpu.make_async_copy(src.at[part], held.at[slot], in_sem.at[slot]))
            out.append(pltpu.make_async_copy(held.at[slot], dst.at[part], out_sem.at[slot]))
    for copy in into:
        copy.start()
    for arrived, copy in zip(into, out):
        arrived.wait()
        copy.start()
    for copy in out:
        copy.wait()


def body(left_modes, right_modes, momenta, far_fields):
    times = lax.axis_size("tm")
    groups = lax.axis_size("site")
    nz = groups // PAIR
    rows, width = left_modes.shape[2:]
    modes, cols = far_fields.shape[2:]
    factor = (2.0 * width * groups) ** (-0.5)
    chunk = (2, rows, cols)
    thin = thin_rows(rows)
    large = (2, rows - thin, cols)
    small = (2, thin, cols)
    dma = pltpu.SemaphoreType.DMA
    meson, product = pl.pallas_call(
        functools.partial(kernel, times, groups, factor),
        out_shape=[jax.ShapeDtypeStruct(chunk, jnp.bfloat16)] * 2,
        in_specs=[
            pl.BlockSpec(memory_space=pl.ANY),
            pl.BlockSpec(memory_space=pl.ANY),
            pl.BlockSpec(memory_space=pltpu.SMEM),
            pl.BlockSpec(memory_space=pl.ANY),
        ],
        out_specs=[pl.BlockSpec(memory_space=pl.ANY)] * 2,
        scratch_shapes=[
            pltpu.VMEM((2 * rows, 2 * width), jnp.bfloat16),
            pltpu.VMEM((2, modes, cols), jnp.bfloat16),
            pltpu.VMEM((nz,) + large, jnp.bfloat16),
            pltpu.VMEM((nz,) + large, jnp.bfloat16),
            pltpu.VMEM((nz,) + large, jnp.bfloat16),
            pltpu.VMEM((nz, 2) + large, jnp.bfloat16),
            pltpu.VMEM((groups,) + chunk, jnp.bfloat16),
            pltpu.VMEM(chunk, jnp.float32),
            dma(()),
            dma(()),
            dma((nz, 2)),
            dma((nz, 2)),
            dma((nz, 2)),
            dma((nz, 2, 2)),
            dma((groups, 2)),
            dma((nz, 2)),
            dma((nz, 2)),
            dma((nz, 2)),
            dma((nz,)),
            dma((nz,)),
            dma((nz,)),
            dma(()),
            pltpu.VMEM((2, width, rows), jnp.bfloat16),
            pltpu.VMEM((groups, 2, width, cols), jnp.bfloat16),
            dma(()),
            dma((groups,)),
            pltpu.VMEM((nz, PAIR) + chunk, jnp.float32),
            pltpu.VMEM((nz, PAIR) + small, jnp.bfloat16),
            pltpu.VMEM((nz, 2, PAIR) + small, jnp.bfloat16),
            dma((nz,)),
            dma((nz, 2)),
            pltpu.VMEM(small, jnp.bfloat16),
            pltpu.VMEM(small, jnp.bfloat16),
            dma((2,)),
            pltpu.VMEM(chunk, jnp.bfloat16),
            dma((3,)),
        ],
        compiler_params=pltpu.CompilerParams(
            collective_id=0, has_side_effects=True, vmem_limit_bytes=60 * 2**20
        ),
    )(
        jnp.swapaxes(left_modes[0], 1, 2),
        jnp.swapaxes(right_modes[0], 1, 2),
        momenta,
        far_fields[0],
    )
    meson, product = pl.pallas_call(
        settle,
        out_shape=[jax.ShapeDtypeStruct(chunk, jnp.bfloat16)] * 2,
        in_specs=[pl.BlockSpec(memory_space=pl.ANY)] * 2,
        out_specs=[pl.BlockSpec(memory_space=pl.ANY)] * 2,
        scratch_shapes=[pltpu.VMEM((4, rows, cols), jnp.bfloat16), dma((4,)), dma((4,))],
        compiler_params=pltpu.CompilerParams(vmem_limit_bytes=60 * 2**20),
    )(meson, product)
    return (meson[None], product[None])


def solution(mesh):
    return jax.shard_map(
        body,
        mesh=mesh,
        in_specs=(
            P("tm", None, None, "site"),
            P("tm", None, None, "site"),
            P("tm", None),
            P("tm", None, None, "site"),
        ),
        out_specs=(P("tm", None, None, "site"), P("tm", None, None, "site")),
        check_vma=False,
    )
```

```python
import functools
import math

import jax
import jax.numpy as jnp
from jax import lax
from jax.experimental import pallas as pl
from jax.experimental.pallas import tpu as pltpu
from jax.sharding import PartitionSpec as P

SC = 12
EXTENT = 96
DT = 3
PAIR = 2
MESH = pl.DeviceIdType.MESH


def block_coords(sites):
    coords = []
    for axis in range(3):
        coord = jnp.zeros_like(sites)
        for level in range(7):
            coord = coord + ((sites >> (3 * level + axis)) & 1) * 2**level
        coords.append(coord)
    return coords


def thin_rows(rows):
    return max(16, rows // 8 // 16 * 16)


def order(k, z, nz):
    short = jnp.minimum(z, nz - 1 - z)
    lone = nz - 1 - 2 * short
    toward = jnp.where(z < nz - 1 - z, 1, -1)
    rest = k - lone
    far = z + toward * (nz - 1 - short - k)
    near = z + (short - rest // 2) * (1 - 2 * (rest % 2))
    return jnp.where(k == nz - 1, z, jnp.where(k < lone, far, near))


def kernel(
    times,
    groups,
    factor,
    left_ref,
    right_ref,
    momenta_ref,
    far_ref,
    meson_ref,
    product_ref,
    phased,
    field,
    x_out,
    x_in,
    z_out,
    z_in,
    gathered,
    total,
    far_send,
    far_recv,
    xo_sem,
    xi_sem,
    zo_sem,
    zi_sem,
    g_recv,
    g_up,
    g_down,
    g_pair,
    s_recv,
    s_up,
    s_down,
    s_pair,
    left_in,
    right_in,
    left_sem,
    right_sem,
    kept,
    t_out,
    t_in,
    to_sem,
    ti_sem,
    m_out,
    m_in,
    m_sem,
    staged,
    leave,
):
    nz = groups // PAIR
    rows, cols = meson_ref.shape[1:]
    width = left_ref.shape[1]
    thin = thin_rows(rows)
    tm = lax.axis_index("tm")
    me = lax.axis_index("site")
    z = me // PAIR
    x = me % PAIR
    mate = z * PAIR + (1 - x)
    up = me + PAIR
    down = me - PAIR
    has_up = z < nz - 1
    has_down = z > 0
    target = lax.rem(tm + times - DT % times, times)
    source = lax.rem(tm + DT, times)

    left_copy = pltpu.make_async_copy(left_ref, left_in, left_sem)
    left_copy.start()

    def right_copy(site):
        lanes = pl.ds(pl.multiple_of(site * cols, cols), cols)
        return pltpu.make_async_copy(right_ref.at[:, :, lanes], right_in.at[site], right_sem.at[site])

    def load(k, carry):
        dest = order(k, z, nz)
        right_copy(dest * PAIR + (1 - x)).start()
        right_copy(dest * PAIR + x).start()
        return carry

    lax.fori_loop(0, nz, load, 0)

    barrier = pltpu.get_barrier_semaphore()
    pl.semaphore_signal(barrier, inc=1, device_id=(target, me), device_id_type=MESH)
    pl.semaphore_signal(barrier, inc=1, device_id=(source, me), device_id_type=MESH)
    pl.semaphore_signal(barrier, inc=1, device_id=(tm, mate), device_id_type=MESH)

    @pl.when(has_up)
    def _():
        pl.semaphore_signal(barrier, inc=1, device_id=(tm, up), device_id_type=MESH)

    @pl.when(has_down)
    def _():
        pl.semaphore_signal(barrier, inc=1, device_id=(tm, down), device_id_type=MESH)

    def send(src, dst, send_sem, recv_sem, site):
        return pltpu.make_async_remote_copy(
            src_ref=src,
            dst_ref=dst,
            send_sem=send_sem,
            recv_sem=recv_sem,
            device_id=(tm, site),
            device_id_type=MESH,
        )

    column = lax.broadcasted_iota(jnp.int32, (width, 128), 0)
    inside = jnp.floor((column.astype(jnp.float32) + 0.5) / SC).astype(jnp.int32)
    sites = me * (width // SC) + inside
    coords = block_coords(sites)
    wave = sum(momenta_ref[0, axis] * coords[axis] for axis in range(3)).astype(jnp.float32)
    wave = wave - EXTENT * jnp.floor((wave + 0.5) / EXTENT)
    angles = 2.0 * math.pi / EXTENT * wave
    cosine = jnp.cos(angles)[:, 0:1]
    sine = jnp.sin(angles)[:, 0:1]
    left_copy.wait()
    real = left_in[0].astype(jnp.float32)
    imag = left_in[1].astype(jnp.float32)
    phased_real = factor * (real * cosine + imag * sine)
    phased_imag = factor * (real * sine - imag * cosine)
    for_real = jnp.concatenate([phased_real, -phased_imag], axis=0)
    for_imag = jnp.concatenate([phased_imag, phased_real], axis=0)
    phased[0:rows, :] = for_real.T.astype(jnp.bfloat16)
    phased[rows : 2 * rows, :] = for_imag.T.astype(jnp.bfloat16)

    pl.semaphore_wait(barrier, 3 + has_up.astype(jnp.int32) + has_down.astype(jnp.int32))

    far_copy = pltpu.make_async_remote_copy(
        src_ref=far_ref,
        dst_ref=field,
        send_sem=far_send,
        recv_sem=far_recv,
        device_id=(target, me),
        device_id_type=MESH,
    )
    far_copy.start()

    def partial(site):
        right_copy(site).wait()
        right = right_in[site].reshape(2 * width, cols)
        both = jnp.dot(phased[...], right, preferred_element_type=jnp.float32)
        return both.reshape(2, rows, cols)

    def x_copy(dest, part):
        return send(
            x_out.at[dest, part],
            x_in.at[dest, part],
            xo_sem.at[dest, part],
            xi_sem.at[dest, part],
            mate,
        )

    def z_copy(dest, part, side, site):
        return send(
            z_out.at[dest, part],
            z_in.at[dest, side, part],
            zo_sem.at[dest, part],
            zi_sem.at[dest, side, part],
            site,
        )

    def t_copy(dest, side, site):
        return send(
            t_out.at[dest], t_in.at[dest, side], to_sem.at[dest], ti_sem.at[dest, side], site
        )

    m_copy = send(m_out, m_in, m_sem.at[0], m_sem.at[1], mate)

    def first(k, carry):
        dest = order(k, z, nz)
        theirs = partial(dest * PAIR + (1 - x))
        for part in range(2):
            x_out[dest, part] = theirs[part, thin:].astype(jnp.bfloat16)
            x_copy(dest, part).start()
        kept[dest, 1, :, :thin] = theirs[:, :thin]
        kept[dest, 0] = partial(dest * PAIR + x)

        @pl.when((dest > z) & has_down)
        def _():
            t_copy(dest, 0, up).wait_recv()
            kept[dest, :, :, :thin] += t_in[dest, 0].astype(jnp.float32)

        @pl.when((dest < z) & has_up)
        def _():
            t_copy(dest, 1, down).wait_recv()
            kept[dest, :, :, :thin] += t_in[dest, 1].astype(jnp.float32)

        @pl.when(dest > z)
        def _():
            t_out[dest] = kept[dest, :, :, :thin].astype(jnp.bfloat16)
            t_copy(dest, 0, up).start()

        @pl.when(dest < z)
        def _():
            t_out[dest] = kept[dest, :, :, :thin].astype(jnp.bfloat16)
            t_copy(dest, 1, down).start()

        return carry

    lax.fori_loop(0, nz, first, 0)

    def block(site):
        return gathered.at[site]

    def slim(ref):
        return ref.at[:, pl.ds(0, thin), :]

    def rest(site, part):
        return gathered.at[site, part, pl.ds(thin, rows - thin), :]

    def pair(site):
        first_of = pl.multiple_of(site // PAIR * PAIR, PAIR)
        return gathered.at[pl.ds(first_of, PAIR), :, pl.ds(0, thin), :]

    def rest_copy(site, part, sem, to):
        src = rest(site, part)
        return send(src, src, sem.at[site // PAIR, part], g_recv.at[site, part], to)

    def to_up(site, part):
        return rest_copy(site, part, g_up, up)

    def to_down(site, part):
        return rest_copy(site, part, g_down, down)

    def to_mate(site, part):
        return rest_copy(site, part, g_pair, mate)

    def second(k, carry):
        dest = order(k, z, nz)
        for part in range(2):
            x_copy(dest, part).wait_recv()
            kept[dest, 0, part, thin:] += x_in[dest, part].astype(jnp.float32)

            @pl.when((dest >= z) & has_down)
            def _():
                z_copy(dest, part, 0, up).wait_recv()
                kept[dest, 0, part, thin:] += z_in[dest, 0, part].astype(jnp.float32)

            @pl.when((dest <= z) & has_up)
            def _():
                z_copy(dest, part, 1, down).wait_recv()
                kept[dest, 0, part, thin:] += z_in[dest, 1, part].astype(jnp.float32)

            @pl.when(dest > z)
            def _():
                z_out[dest, part] = kept[dest, 0, part, thin:].astype(jnp.bfloat16)
                z_copy(dest, part, 0, up).start()

            @pl.when(dest < z)
            def _():
                z_out[dest, part] = kept[dest, 0, part, thin:].astype(jnp.bfloat16)
                z_copy(dest, part, 1, down).start()

            @pl.when(dest == z)
            def _():
                gathered[me, part, thin:] = kept[z, 0, part, thin:].astype(jnp.bfloat16)

                @pl.when(has_up)
                def _():
                    to_up(me, part).start()

                @pl.when(has_down)
                def _():
                    to_down(me, part).start()

                to_mate(me, part).start()

        @pl.when(k == 0)
        def _():
            @pl.when(has_down)
            def _():
                t_copy(z, 0, up).wait_recv()
                kept[z, :, :, :thin] += t_in[z, 0].astype(jnp.float32)

            @pl.when(has_up)
            def _():
                t_copy(z, 1, down).wait_recv()
                kept[z, :, :, :thin] += t_in[z, 1].astype(jnp.float32)

            m_out[...] = kept[z, 1, :, :thin].astype(jnp.bfloat16)
            m_copy.start()

        return carry

    lax.fori_loop(0, nz, second, 0)
    m_copy.wait_recv()
    kept[z, 0, :, :thin] += m_in[...].astype(jnp.float32)
    gathered[me, :, :thin] = kept[z, 0, :, :thin].astype(jnp.bfloat16)

    def slim_up(site):
        line = site // PAIR
        return send(pair(site), pair(site), s_up.at[line], s_recv.at[line], up)

    def slim_down(site):
        line = site // PAIR
        return send(pair(site), pair(site), s_down.at[line], s_recv.at[line], down)

    def slim_mate(site):
        return send(slim(block(site)), slim(block(site)), s_pair, s_recv.at[z], mate)

    own = block(me)
    slim_mate(me).start()
    meson_copy = pltpu.make_async_copy(own, meson_ref, leave.at[0])
    meson_copy.start()

    slim_mate(mate).wait_recv()

    @pl.when((z == 0) & has_up)
    def _():
        slim_up(me).start()

    @pl.when((z == nz - 1) & has_down)
    def _():
        slim_down(me).start()

    far_copy.wait()

    def gain(value, site):
        lines = pl.ds(pl.multiple_of(site * cols, cols), cols)
        both = value[...].reshape(2 * rows, cols)

        def dot(part):
            whole = jnp.dot(both, field[part, lines, :], preferred_element_type=jnp.float32)
            return whole[:rows], whole[rows:]

        real_real, imag_real = dot(0)
        real_imag, imag_imag = dot(1)
        return (real_real - imag_imag, real_imag + imag_real)

    for part, value in enumerate(gain(own, me)):
        total[part] = value

    def arrive(site):
        for part, value in enumerate(gain(block(site), site)):
            total[part] += value

    def relay(d, carry):
        below = me - d * PAIR
        above = me + d * PAIR

        for part in range(2):

            @pl.when(z >= d)
            def _():
                to_up(below, part).wait_recv()

                @pl.when(has_up)
                def _():
                    to_up(below, part).start()

                to_mate(below, part).start()

            @pl.when(z + d < nz)
            def _():
                to_down(above, part).wait_recv()

                @pl.when(has_down)
                def _():
                    to_down(above, part).start()

                to_mate(above, part).start()

        @pl.when((z == d) & has_up)
        def _():
            slim_up(me).start()

        @pl.when((z + d == nz - 1) & has_down)
        def _():
            slim_down(me).start()

        return carry

    lax.fori_loop(1, nz, relay, 0)

    def thins(d, carry):
        below = me - d * PAIR
        above = me + d * PAIR

        @pl.when(z >= d)
        def _():
            slim_up(below).wait_recv()

            @pl.when(has_up)
            def _():
                slim_up(below).start()

        @pl.when(z + d < nz)
        def _():
            slim_down(above).wait_recv()

            @pl.when(has_down)
            def _():
                slim_down(above).start()

        @pl.when(z >= d)
        def _():
            arrive(below)

        @pl.when(z + d < nz)
        def _():
            arrive(above)

        return carry

    lax.fori_loop(1, nz, thins, 0)

    def across(d, carry):
        @pl.when(z >= d)
        def _():
            site = mate - d * PAIR
            to_mate(site, 0).wait_recv()
            to_mate(site, 1).wait_recv()
            arrive(site)

        @pl.when((z + d < nz) & (d > 0))
        def _():
            site = mate + d * PAIR
            to_mate(site, 0).wait_recv()
            to_mate(site, 1).wait_recv()
            arrive(site)

        return carry

    lax.fori_loop(0, nz, across, 0)
    copies = [meson_copy]
    for part in range(2):
        staged[part] = total[part].astype(jnp.bfloat16)
        copy = pltpu.make_async_copy(staged.at[part], product_ref.at[part], leave.at[1 + part])
        copy.start()
        copies.append(copy)

    def drain(k, carry):
        for part in range(2):
            x_copy(k, part).wait_send()
            to_mate(k * PAIR + x, part).wait_send()

            @pl.when(k != z)
            def _():
                z_copy(k, part, 0, mate).wait_send()

            @pl.when((k <= z) & has_up)
            def _():
                to_up(k * PAIR + x, part).wait_send()

            @pl.when((k >= z) & has_down)
            def _():
                to_down(k * PAIR + x, part).wait_send()

        @pl.when(k != z)
        def _():
            t_copy(k, 0, mate).wait_send()

        @pl.when((k <= z) & has_up)
        def _():
            slim_up(k * PAIR).wait_send()

        @pl.when((k >= z) & has_down)
        def _():
            slim_down(k * PAIR).wait_send()

        return carry

    lax.fori_loop(0, nz, drain, 0)
    slim_mate(me).wait_send()
    m_copy.wait_send()
    for copy in copies:
        copy.wait()


def settle(meson_in, product_in, meson_ref, product_ref, held, in_sem, out_sem):
    parts = meson_in.shape[0]
    pairs = [(meson_in, meson_ref), (product_in, product_ref)]
    into, out = [], []
    for which, (src, dst) in enumerate(pairs):
        for part in range(parts):
            slot = which * parts + part
            into.append(pltpu.make_async_copy(src.at[part], held.at[slot], in_sem.at[slot]))
            out.append(pltpu.make_async_copy(held.at[slot], dst.at[part], out_sem.at[slot]))
    for copy in into:
        copy.start()
    for arrived, copy in zip(into, out):
        arrived.wait()
        copy.start()
    for copy in out:
        copy.wait()


def body(left_modes, right_modes, momenta, far_fields):
    times = lax.axis_size("tm")
    groups = lax.axis_size("site")
    nz = groups // PAIR
    rows, width = left_modes.shape[2:]
    modes, cols = far_fields.shape[2:]
    factor = (2.0 * width * groups) ** (-0.5)
    chunk = (2, rows, cols)
    thin = thin_rows(rows)
    large = (2, rows - thin, cols)
    small = (2, thin, cols)
    dma = pltpu.SemaphoreType.DMA
    meson, product = pl.pallas_call(
        functools.partial(kernel, times, groups, factor),
        out_shape=[jax.ShapeDtypeStruct(chunk, jnp.bfloat16)] * 2,
        in_specs=[
            pl.BlockSpec(memory_space=pl.ANY),
            pl.BlockSpec(memory_space=pl.ANY),
            pl.BlockSpec(memory_space=pltpu.SMEM),
            pl.BlockSpec(memory_space=pl.ANY),
        ],
        out_specs=[pl.BlockSpec(memory_space=pl.ANY)] * 2,
        scratch_shapes=[
            pltpu.VMEM((2 * rows, 2 * width), jnp.bfloat16),
            pltpu.VMEM((2, modes, cols), jnp.bfloat16),
            pltpu.VMEM((nz,) + large, jnp.bfloat16),
            pltpu.VMEM((nz,) + large, jnp.bfloat16),
            pltpu.VMEM((nz,) + large, jnp.bfloat16),
            pltpu.VMEM((nz, 2) + large, jnp.bfloat16),
            pltpu.VMEM((groups,) + chunk, jnp.bfloat16),
            pltpu.VMEM(chunk, jnp.float32),
            dma(()),
            dma(()),
            dma((nz, 2)),
            dma((nz, 2)),
            dma((nz, 2)),
            dma((nz, 2, 2)),
            dma((groups, 2)),
            dma((nz, 2)),
            dma((nz, 2)),
            dma((nz, 2)),
            dma((nz,)),
            dma((nz,)),
            dma((nz,)),
            dma(()),
            pltpu.VMEM((2, width, rows), jnp.bfloat16),
            pltpu.VMEM((groups, 2, width, cols), jnp.bfloat16),
            dma(()),
            dma((groups,)),
            pltpu.VMEM((nz, PAIR) + chunk, jnp.float32),
            pltpu.VMEM((nz, PAIR) + small, jnp.bfloat16),
            pltpu.VMEM((nz, 2, PAIR) + small, jnp.bfloat16),
            dma((nz,)),
            dma((nz, 2)),
            pltpu.VMEM(small, jnp.bfloat16),
            pltpu.VMEM(small, jnp.bfloat16),
            dma((2,)),
            pltpu.VMEM(chunk, jnp.bfloat16),
            dma((3,)),
        ],
        compiler_params=pltpu.CompilerParams(
            collective_id=0, has_side_effects=True, vmem_limit_bytes=60 * 2**20
        ),
    )(
        jnp.swapaxes(left_modes[0], 1, 2),
        jnp.swapaxes(right_modes[0], 1, 2),
        momenta,
        far_fields[0],
    )
    meson, product = pl.pallas_call(
        settle,
        out_shape=[jax.ShapeDtypeStruct(chunk, jnp.bfloat16)] * 2,
        in_specs=[pl.BlockSpec(memory_space=pl.ANY)] * 2,
        out_specs=[pl.BlockSpec(memory_space=pl.ANY)] * 2,
        scratch_shapes=[pltpu.VMEM((4, rows, cols), jnp.bfloat16), dma((4,)), dma((4,))],
        compiler_params=pltpu.CompilerParams(vmem_limit_bytes=60 * 2**20),
    )(meson, product)
    return (meson[None], product[None])


def solution(mesh):
    return jax.shard_map(
        body,
        mesh=mesh,
        in_specs=(
            P("tm", None, None, "site"),
            P("tm", None, None, "site"),
            P("tm", None),
            P("tm", None, None, "site"),
        ),
        out_specs=(P("tm", None, None, "site"), P("tm", None, None, "site")),
        check_vma=False,
    )
```
